32 devices in a mesh: az: 8 (over z, x), rad: 4 (over y, core).
Axes of the slice: x: 2, y: 2, z: 4, core: 2. Of those that a mesh axis runs over, the one named last changes fastest.
Arguments:
- state: bfloat16 [4, 64, 2048, 512], P(None, None, 'az', 'rad'), may hold values from -6 to 6
- source: bfloat16 [64, 2048, 512], P(None, 'az', 'rad'), may hold values from -6 to 6
- shear: bfloat16 [64, 2048, 512], P(None, 'az', 'rad'), may hold values from 0.5 to 4
- permeability: bfloat16 [64, 2048, 512], P(None, 'az', 'rad'), may hold values from 0.099609375 to 10
- radial_basis: float32 [512, 512], P('rad'), may hold values from -1 to 2
- radial_eigen: float32 [512], replicated, may hold values from 4e-05 to 4
Outputs:
- correction: bfloat16 [4, 64, 2048, 512], P(None, None, 'az', 'rad')
The draws below stay inside these ranges and needn't reach their ends.
All inputs are finite; a program needn't handle non-finite values.
Results may differ from the reference program's by a relative error of at most 0.001.
Values may be sent and summed in bfloat16 or wider, within the bound.
No kernel may reach another device: no remote copies, remote signals or barrier semaphores. Data moves between devices by JAX's collectives and lax.ppermute only.
A program may use at most 384 MiB of HBM per device.

```python
import math
import jax
import jax.numpy as jnp
from jax import lax

NH = 64
NA = 2048
NR = 512


def draw_state(key, part):
    azimuth = jnp.arange(NA, dtype=jnp.float32) / NA
    radius = jnp.arange(NR, dtype=jnp.float32) / NR
    jitter = jax.random.truncated_normal(key, -4.0, 4.0, (4, NH, NA, NR), jnp.float32)
    weight = 0.05 * (10.0 ** azimuth)[:, None] * (3.0 ** radius)[None, :]
    values = weight * jitter
    return values.astype(jnp.bfloat16)


def draw_radial_basis(key, part):
    identity = jnp.eye(NR, dtype=jnp.float32)
    jitter = jax.random.truncated_normal(key, -4.0, 4.0, (NR, NR), jnp.float32) * (0.3 / math.sqrt(NR))
    return identity + jitter


def block_scale(rng, shape, cuts, low, top_value):
    factor_of, own = 1.0, jax.random.fold_in(rng, 6)
    for dim, blocks in cuts:
        steps = jnp.exp(jax.random.uniform(jax.random.fold_in(own, dim), (blocks,), jnp.float32, low / len(cuts), top_value / len(cuts)))
        factor_of = factor_of * jnp.repeat(steps, shape[dim] // blocks).reshape([-1 if axis == dim else 1 for axis in range(len(shape))])
    return factor_of


def noise(key, shape, scale, most, shards=(), kind=jnp.bfloat16):
    values = scale * jax.random.normal(key, shape, jnp.float32)
    if shards:
        values = values * block_scale(key, shape, shards, -0.22, 0.18)
    return jnp.clip(values, -most, most).astype(kind)


def setup_inputs(seed: int = 0) -> dict:
    keys = jax.random.split(jax.random.key(seed), 7)
    return {
        "state": draw_state(jax.random.fold_in(keys[6], 71), 0),
        "source": noise(keys[1], (NH, NA, NR), 1.0, 6.0, ((1, 8), (2, 4))),
        "shear": jnp.clip(jnp.exp(math.log(4.0) - 2.0794415 * jax.random.uniform(keys[2], (NH, NA, NR), jnp.float32) ** block_scale(keys[2], (NH, NA, NR), ((1, 8), (2, 4)), -0.2, 0.2)), 0.5, 4.0).astype(jnp.bfloat16),
        "permeability": jnp.clip(jnp.exp(math.log(10.0) - 4.609084 * jax.random.uniform(keys[3], (NH, NA, NR), jnp.float32) ** block_scale(keys[3], (NH, NA, NR), ((1, 8), (2, 4)), -0.2, 0.2)), 0.099609375, 10.0).astype(jnp.bfloat16),
        "radial_basis": draw_radial_basis(jax.random.fold_in(keys[6], 71), 0),
        "radial_eigen": jnp.clip(jnp.exp(jax.random.uniform(keys[5], (NR,), jnp.float32, math.log(3.9999998989515007e-05), math.log(4.0))), 3.9999998989515007e-05, 4.0),
    }


biot_coupling = 2.0
storage = 1.0

def neighbor(extended, grid_axis, offset):
    lead = extended.ndim - 3
    window = [slice(None)] * lead + [slice(1, -1)] * 3
    length = extended.shape[lead + grid_axis]
    window[lead + grid_axis] = slice(1 + offset, length - 1 + offset)
    return extended[tuple(window)]

def stencil(extended, source_block):
    center = neighbor(extended, 0, 0)
    diagonal = jnp.zeros_like(center[4])
    momentum = [jnp.zeros_like(center[0]), jnp.zeros_like(center[0]), jnp.zeros_like(center[0])]
    fluid = jnp.zeros_like(center[0])
    for grid_axis in (0, 1, 2):
        for offset in (1, -1):
            beside = neighbor(extended, grid_axis, offset)
            shear_face = 0.5 * (center[4] + beside[4])
            flow_face = 0.5 * (center[5] + beside[5])
            diagonal = diagonal + shear_face
            momentum = [momentum[channel] + shear_face * (center[channel] - beside[channel]) for channel in range(3)]
            fluid = fluid + flow_face * (center[3] - beside[3])
    component_axes = (2, 1, 0)
    pressure = extended[3]
    spread = jnp.zeros_like(center[0])
    parts = []
    for channel in range(3):
        grid_axis = component_axes[channel]
        gradient = 0.5 * (neighbor(pressure, grid_axis, 1) - neighbor(pressure, grid_axis, -1))
        parts.append(-(momentum[channel] + biot_coupling * gradient))
        member = extended[channel]
        spread = spread + 0.5 * (neighbor(member, grid_axis, 1) - neighbor(member, grid_axis, -1))
    parts.append(source_block + biot_coupling * spread + storage * center[3] + fluid)
    return (jnp.stack(parts), diagonal)

def cosine_table(extent):
    row_ids = jnp.arange(extent, dtype=jnp.float32)[:, None]
    col_ids = jnp.arange(extent, dtype=jnp.float32)[None, :]
    scaled = jnp.where(row_ids == 0, math.sqrt(1.0 / extent), math.sqrt(2.0 / extent))
    return scaled * jnp.cos(math.pi * (col_ids + 0.5) * row_ids / extent)

def precondition(residual_p, radial_basis, radial_eigen):
    highest = lax.Precision.HIGHEST
    cosine = cosine_table(NH)
    heights = jnp.einsum('lh,har->lar', cosine, residual_p, precision=highest, preferred_element_type=jnp.float32)
    levels = jnp.arange(NH, dtype=jnp.float32)
    height_eigen = 4.0 * jnp.sin(math.pi * levels / (2.0 * NH)) ** 2
    waves = jnp.arange(NA, dtype=jnp.float32)
    azimuth_eigen = 4.0 * jnp.sin(math.pi * waves / NA) ** 2

    def mode_block(inputs):
        plane, level_eigen = inputs
        coeffs = jnp.dot(plane, radial_basis, precision=highest, preferred_element_type=jnp.float32)
        spectral = jnp.fft.fft(coeffs, axis=0)
        totals = storage + radial_eigen[None, :] + level_eigen + azimuth_eigen[:, None]
        solved = jnp.real(jnp.fft.ifft(spectral / totals, axis=0))
        return jnp.dot(solved, radial_basis.T, precision=highest, preferred_element_type=jnp.float32)
    planes = lax.map(mode_block, (heights, height_eigen))
    return jnp.einsum('lh,lar->har', cosine, planes, precision=highest, preferred_element_type=jnp.float32)

def reference(state, source, shear, permeability, radial_basis, radial_eigen):
    layers = jnp.concatenate([state, shear[None], permeability[None]], axis=0)
    layers = jnp.pad(layers, ((0, 0), (1, 1), (0, 0), (1, 1)))
    layers = jnp.concatenate([layers[:, :, -1:], layers, layers[:, :, :1]], axis=2)
    slab_rows = math.gcd(NH, 8)

    def slab(block_index):
        first_row = block_index * slab_rows
        window_part = lax.dynamic_slice_in_dim(layers, first_row, slab_rows + 2, 1).astype(jnp.float32)
        source_part = lax.dynamic_slice_in_dim(source, first_row, slab_rows, 0).astype(jnp.float32)
        residual, diagonal = stencil(window_part, source_part)
        moment_step = residual[:3] / diagonal
        return (moment_step, residual[3], jnp.sum(residual[:3] * residual[:3]), jnp.sum(residual[:3] * moment_step))
    steps, fluid_rows, square_parts, cross_parts = lax.map(slab, jnp.arange(NH // slab_rows, dtype=jnp.int32))
    moment_step = jnp.moveaxis(steps, 0, 1).reshape(3, NH, NA, NR)
    residual_p = fluid_rows.reshape(NH, NA, NR)
    press_step = precondition(residual_p, radial_basis, radial_eigen)
    total_rr = jnp.sum(square_parts) + jnp.sum(residual_p * residual_p)
    total_rz = jnp.sum(cross_parts) + jnp.sum(residual_p * press_step)
    alpha = total_rr / total_rz
    return jnp.concatenate([(alpha * moment_step).astype(jnp.bfloat16), (alpha * press_step).astype(jnp.bfloat16)[None]], axis=0)
```

```python
import math

import jax
import jax.numpy as jnp
from jax import lax
from jax.experimental import pallas as pl
from jax.experimental.pallas import tpu as pltpu
from jax.sharding import PartitionSpec as P


biot_coupling = 2.0
storage = 1.0

f32 = jnp.float32
bf16 = jnp.bfloat16


SLAB = 8
ROWS = 32
TILE = 32
CHUNKS = 2


def params(limit=56):
    return pltpu.CompilerParams(
        dimension_semantics=("arbitrary",), vmem_limit_bytes=limit * 1024 * 1024
    )


def lanes_of(shape):
    return lax.broadcasted_iota(jnp.int32, shape, len(shape) - 1)


def split(x):
    high = x.astype(bf16)
    low = (x - high.astype(f32)).astype(bf16)
    return high, low


def fold(x):
    total = x[0:8]
    for start in range(8, x.shape[0], 8):
        total = total + x[start : start + 8]
    return total


def split_table(x):
    rounded = lax.reduce_precision(x, exponent_bits=8, mantissa_bits=7)
    return rounded.astype(bf16), (x - rounded).astype(bf16)


def edges_kernel(*refs):
    top_ref, end_ref = refs[:2]
    fields = refs[2:5]
    cols_ref, first_ref, last_ref, acc = refs[5:]
    step = pl.program_id(0)
    slab, count, width = fields[2].shape
    rows = min(64, count)
    lane = lanes_of((rows, width))
    for c in range(3):
        src = fields[c].at[0] if len(fields[c].shape) == 4 else fields[c]
        for start in range(0, count, rows):
            value = acc[c, start : start + rows, :]
            for i in range(slab):
                h = step * slab + i
                x = src[i, start : start + rows, :].astype(f32)
                value = jnp.where((lane >> 1) == h, pltpu.roll(x, 2 * h + 1, 1), value)
                if c and start == 0:
                    first_ref[c, pl.ds(h, 1), :] = x[0:1]
                if c and start + rows == count:
                    last_ref[c, pl.ds(h, 1), :] = x[rows - 1 : rows]
            acc[c, start : start + rows, :] = value
    for i in range(slab):
        h = step * slab + i
        strip = end_ref.shape[2]
        first_ref[0, pl.ds(h, 1), :] = top_ref[0, i].astype(f32)[0:1]
        last_ref[0, pl.ds(h, 1), :] = end_ref[0, i].astype(f32)[strip - 1 : strip]

    @pl.when(step == pl.num_programs(0) - 1)
    def _():
        for c in range(3):
            for start in range(0, count, rows):
                v = acc[c, start : start + rows, :]
                swapped = jnp.where(lane % 2 == 0, pltpu.roll(v, width - 1, 1), pltpu.roll(v, 1, 1))
                cols_ref[c, start : start + rows, :] = swapped.astype(bf16)


def edges(state, coefficient, row_only, channels):
    _, height, count, width = state.shape
    strip = 16
    whole = lambda *shape: pl.BlockSpec(shape, lambda i: (0,) * len(shape))
    full = lambda c: pl.BlockSpec((1, SLAB, count, width), lambda i: (c, i, 0, 0))
    return pl.pallas_call(
        edges_kernel,
        grid=(height // SLAB,),
        in_specs=[
            pl.BlockSpec((1, SLAB, strip, width), lambda i: (row_only, i, 0, 0)),
            pl.BlockSpec((1, SLAB, strip, width), lambda i: (row_only, i, count // strip - 1, 0)),
            full(channels[0]),
            full(channels[1]),
            pl.BlockSpec((SLAB, count, width), lambda i: (i, 0, 0)),
        ],
        out_specs=[whole(3, count, width), whole(3, height, width), whole(3, height, width)],
        out_shape=[
            jax.ShapeDtypeStruct((3, count, width), bf16),
            jax.ShapeDtypeStruct((3, height, width), f32),
            jax.ShapeDtypeStruct((3, height, width), f32),
        ],
        scratch_shapes=[pltpu.VMEM((3, count, width), f32)],
        compiler_params=params(),
        name="edges",
    )(state, state, state, state, coefficient)


def neighbours(cols, first, last):
    n_rad = lax.axis_size("rad")
    n_az = lax.axis_size("az")
    from_right = lax.ppermute(cols, "rad", [(i + 1, i) for i in range(n_rad - 1)])
    from_left = lax.ppermute(cols, "rad", [(i, i + 1) for i in range(n_rad - 1)])
    before = lax.ppermute(last, "az", [(i, (i + 1) % n_az) for i in range(n_az)])
    after = lax.ppermute(first, "az", [((i + 1) % n_az, i) for i in range(n_az)])
    beside = jnp.where(lanes_of(cols.shape) % 2 == 0, from_right, from_left)
    return beside, before, after


def stage(scratch, center, above, below, before, after, step, steps, slab, count):
    top = jnp.where(step > 0, 1.0, 0.0)
    bottom = jnp.where(step < steps - 1, 1.0, 0.0)
    scratch[0, 8 : 8 + count, :] = above[...].astype(f32) * top
    scratch[slab + 1, 8 : 8 + count, :] = below[...].astype(f32) * bottom
    for i in range(slab):
        scratch[i + 1, 8 : 8 + count, :] = center[i].astype(f32)
        if before is not None:
            h = step * slab + i
            scratch[i + 1, 7:8, :] = before[pl.ds(h, 1), :]
            scratch[i + 1, 8 + count : 9 + count, :] = after[pl.ds(h, 1), :]


def radial_pair(x, beside, lane):
    width = x.shape[1]
    right = jnp.where(lane == width - 1, beside, pltpu.roll(x, width - 1, 1))
    left = jnp.where(lane == 0, beside, pltpu.roll(x, 1, 1))
    return right, left


def fluid_kernel(
    p_ref, p_up, p_dn, k_ref, k_up, k_dn, z_ref, z_up, z_dn, r_ref, t_ref, src_ref,
    beside_ref, before_ref, after_ref, cos_ref,
    *rest,
):
    outs, (sum_ref, ps, ks, zs, ts, res) = rest[:-6], rest[-6:]
    step = pl.program_id(0)
    slab, count, width = src_ref.shape
    height = before_ref.shape[1]
    steps = height // slab
    tile, levels, _ = outs[0].shape

    @pl.when(step == 0)
    def _():
        sum_ref[...] = jnp.zeros_like(sum_ref)

    @pl.when(step < steps)
    def _():
        stage(ps, p_ref.at[0], p_up.at[0, 0], p_dn.at[0, 0], before_ref.at[1], after_ref.at[1], step, steps, slab, count)
        stage(ks, k_ref, k_up.at[0], k_dn.at[0], before_ref.at[2], after_ref.at[2], step, steps, slab, count)
        stage(zs, z_ref.at[0], z_up.at[0, 0], z_dn.at[0, 0], None, None, step, steps, slab, count)
        for i in range(slab):
            h = step * slab + i
            ts[i, 8 : 8 + count, :] = t_ref[0, i].astype(f32)
            ts[i, 7:8, :] = before_ref[0, pl.ds(h, 1), :]
            ts[i, 8 + count : 9 + count, :] = after_ref[0, pl.ds(h, 1), :]
        lane = lanes_of((ROWS, width))

        def plane(i, total):
            h = step * slab + i
            shift = 2 * height - 1 - 2 * h
            for a in range(0, count, ROWS):
                at = slice(8 + a, 8 + a + ROWS)
                prev = slice(7 + a, 7 + a + ROWS)
                nxt = slice(9 + a, 9 + a + ROWS)
                own = slice(a, a + ROWS)
                p = ps[i + 1, at, :]
                k = ks[i + 1, at, :]
                nb = [pltpu.roll(beside_ref[c, own, :].astype(f32), shift, 1) for c in range(3)]
                p_r, p_l = radial_pair(p, nb[1], lane)
                k_r, k_l = radial_pair(k, nb[2], lane)
                flux = (k + k_r) * (p - p_r) + (k + k_l) * (p - p_l)
                flux += (k + ks[i + 1, nxt, :]) * (p - ps[i + 1, nxt, :])
                flux += (k + ks[i + 1, prev, :]) * (p - ps[i + 1, prev, :])
                flux += (k + ks[i + 2, at, :]) * (p - ps[i + 2, at, :])
                flux += (k + ks[i, at, :]) * (p - ps[i, at, :])
                u_r, u_l = radial_pair(r_ref[0, i, own, :].astype(f32), nb[0], lane)
                spread = (u_r - u_l) + (ts[i, nxt, :] - ts[i, prev, :])
                spread += zs[i + 2, at, :] - zs[i, at, :]
                value = src_ref[i, own, :].astype(f32) + (0.5 * biot_coupling) * spread
                value = value + storage * p + 0.5 * flux
                res[pl.ds(pl.multiple_of(h * count + a, ROWS), ROWS), :] = value
                total = total + fold(value * value)
            return total

        sum_ref[...] += lax.fori_loop(0, slab, plane, jnp.zeros((8, width), f32))

    @pl.when(step >= steps)
    def _():
        base = (step - steps) * tile

        def pair(j, carry):
            highs, lows = [], []
            for s in range(2):
                x = res[pl.ds(base + 2 * j + s, height, stride=count), :]
                high, low = split(x)
                highs.append(high)
                lows.append(low)
            high = jnp.concatenate(highs, axis=1)
            low = jnp.concatenate(lows, axis=1)
            stacked = jnp.concatenate([high, low, high], axis=0)
            y = jnp.dot(cos_ref[...], stacked, preferred_element_type=f32)
            for s in range(2):
                for block, out in enumerate(outs):
                    out[2 * j + s, :, :] = y[
                        block * levels : (block + 1) * levels, s * width : (s + 1) * width
                    ]
            return carry

        lax.fori_loop(0, tile // 2, pair, 0, unroll=4)


def plane_specs(channel, slab, steps, count, width):
    last = steps * slab - 1
    at = lambda i: jnp.minimum(i, steps - 1)
    up = lambda i: jnp.maximum(at(i) * slab - 1, 0)
    down = lambda i: jnp.minimum(at(i) * slab + slab, last)
    if channel is None:
        return [
            pl.BlockSpec((slab, count, width), lambda i: (at(i), 0, 0)),
            pl.BlockSpec((1, count, width), lambda i: (up(i), 0, 0)),
            pl.BlockSpec((1, count, width), lambda i: (down(i), 0, 0)),
        ]
    return [
        pl.BlockSpec((1, slab, count, width), lambda i: (channel, at(i), 0, 0)),
        pl.BlockSpec((1, 1, count, width), lambda i: (channel, up(i), 0, 0)),
        pl.BlockSpec((1, 1, count, width), lambda i: (channel, down(i), 0, 0)),
    ]


def fluid(state, source, perm, beside, before, after, cosine, pieces):
    _, height, count, width = state.shape
    steps = height // SLAB
    tile = min(TILE, count)
    levels = height // pieces
    specs = lambda c: plane_specs(c, SLAB, steps, count, width)
    whole = lambda x: pl.BlockSpec(x.shape, lambda i: (0,) * x.ndim)
    high, low = split_table(cosine)
    table = jnp.concatenate([high, high, low], axis=1)
    return pl.pallas_call(
        fluid_kernel,
        grid=(steps + count // tile,),
        in_specs=[
            *specs(3), *specs(None), *specs(2), specs(0)[0], specs(1)[0], specs(None)[0],
            whole(beside), whole(before), whole(after), whole(table),
        ],
        out_specs=[
            *[pl.BlockSpec((tile, levels, width), lambda i: (jnp.maximum(i - steps, 0), 0, 0))] * pieces,
            pl.BlockSpec((8, width), lambda i: (0, 0)),
        ],
        out_shape=[
            *[jax.ShapeDtypeStruct((count, levels, width), f32)] * pieces,
            jax.ShapeDtypeStruct((8, width), f32),
        ],
        scratch_shapes=[
            pltpu.VMEM((SLAB + 2, count + 16, width), f32),
            pltpu.VMEM((SLAB + 2, count + 16, width), f32),
            pltpu.VMEM((SLAB + 2, count + 16, width), f32),
            pltpu.VMEM((SLAB, count + 16, width), f32),
            pltpu.VMEM((height * count, width), f32),
        ],
        compiler_params=params(),
        name="fluid",
    )(state, state, state, perm, perm, perm, state, state, state, state, state, source,
      beside, before, after, table)


def momentum_kernel(*refs):
    fields = [refs[3 * c : 3 * c + 3] for c in range(5)]
    fluid_edges, solid_edges = refs[15:18], refs[18:21]
    besides = [e[0].at[c] for e, c in zip([fluid_edges, solid_edges, solid_edges, fluid_edges, solid_edges], (0, 0, 1, 1, 2))]
    row_edges = [solid_edges, fluid_edges, solid_edges, fluid_edges, solid_edges]
    befores = [e[1].at[c] for e, c in zip(row_edges, (0, 0, 1, 1, 2))]
    afters = [e[2].at[c] for e, c in zip(row_edges, (0, 0, 1, 1, 2))]
    out_ref, rr_ref, rz_ref = refs[21:24]
    scratch = refs[24:29]
    step = pl.program_id(0)
    steps = pl.num_programs(0)
    _, slab, count, width = out_ref.shape
    height = fluid_edges[1].shape[1]

    @pl.when(step == 0)
    def _():
        rr_ref[...] = jnp.zeros_like(rr_ref)
        rz_ref[...] = jnp.zeros_like(rz_ref)

    for c in range(5):
        center, up, down = fields[c]
        if c < 4:
            center, up, down = center.at[0], up.at[0, 0], down.at[0, 0]
        else:
            up, down = up.at[0], down.at[0]
        stage(scratch[c], center, up, down, befores[c], afters[c], step, steps, slab, count)
    lane = lanes_of((ROWS, width))

    def plane(i, totals):
        rr, rz = totals
        h = step * slab + i
        shift = 2 * height - 1 - 2 * h
        for a in range(0, count, ROWS):
            at = slice(8 + a, 8 + a + ROWS)
            prev = slice(7 + a, 7 + a + ROWS)
            nxt = slice(9 + a, 9 + a + ROWS)
            own = slice(a, a + ROWS)

            def around(c):
                s = scratch[c]
                x = s[i + 1, at, :]
                nb = pltpu.roll(besides[c][own, :].astype(f32), shift, 1)
                right, left = radial_pair(x, nb, lane)
                return x, (right, left, s[i + 1, nxt, :], s[i + 1, prev, :], s[i + 2, at, :], s[i, at, :])

            g, g_around = around(4)
            faces = [g + other for other in g_around]
            diagonal = faces[0]
            for face in faces[1:]:
                diagonal = diagonal + face
            inverse = 1.0 / diagonal
            _, p = around(3)
            for c in range(3):
                u, u_around = around(c)
                moment = faces[0] * (u - u_around[0])
                for face, other in zip(faces[1:], u_around[1:]):
                    moment = moment + face * (u - other)
                gradient = p[2 * c] - p[2 * c + 1]
                value = -(0.5 * moment + (0.5 * biot_coupling) * gradient)
                step_c = (2.0 * value) * inverse
                out_ref[c, i, own, :] = step_c
                rr = rr + fold(value * value)
                rz = rz + fold(value * step_c)
        return rr, rz

    zero = jnp.zeros((8, width), f32)
    rr, rz = lax.fori_loop(0, slab, plane, (zero, zero))
    rr_ref[...] += rr
    rz_ref[...] += rz


def momentum(state, shear, fluid_edges, solid_edges):
    _, height, count, width = state.shape
    steps = height // SLAB
    specs = lambda c: plane_specs(c, SLAB, steps, count, width)
    whole = lambda x: pl.BlockSpec(x.shape, lambda i: (0,) * x.ndim)
    return pl.pallas_call(
        momentum_kernel,
        grid=(steps,),
        in_specs=[
            *specs(0), *specs(1), *specs(2), *specs(3), *specs(None),
            *[whole(x) for x in (*fluid_edges, *solid_edges)],
        ],
        out_specs=[
            pl.BlockSpec((3, SLAB, count, width), lambda i: (0, i, 0, 0)),
            pl.BlockSpec((8, width), lambda i: (0, 0)),
            pl.BlockSpec((8, width), lambda i: (0, 0)),
        ],
        out_shape=[
            jax.ShapeDtypeStruct((3, height, count, width), f32),
            jax.ShapeDtypeStruct((8, width), f32),
            jax.ShapeDtypeStruct((8, width), f32),
        ],
        scratch_shapes=[pltpu.VMEM((SLAB + 2, count + 16, width), f32)] * 5,
        compiler_params=params(),
        name="momentum",
    )(*[state] * 12, shear, shear, shear, *fluid_edges, *solid_edges)


def product(x, high_ref, low_ref):
    high, low = split(x)
    y = jnp.dot(high, high_ref[...], preferred_element_type=f32)
    y = y + jnp.dot(low, high_ref[...], preferred_element_type=f32)
    return y + jnp.dot(high, low_ref[...], preferred_element_type=f32)


def modes_kernel(*refs):
    slabs, (high_ref, low_ref, ratio_ref, x_ref, all_ref, ends_ref, power) = refs[:-7], refs[-7:]
    step = pl.program_id(0)
    tile, levels, width = slabs[0].shape

    @pl.when(step == 0)
    def _():
        ends_ref[...] = jnp.zeros_like(ends_ref)
        power[...] = jnp.ones_like(power)

    lines = jnp.concatenate([slab[...].reshape(tile * levels, width) for slab in slabs], axis=1)
    y = product(lines, high_ref, low_ref)
    x_ref[...] = y.reshape(x_ref.shape)
    ratio = ratio_ref[...]

    def scan(a, carry):
        forward, backward, weight = carry
        x = x_ref[a]
        return x + ratio * forward, backward + weight * x, weight * ratio

    forward, backward, weight = lax.fori_loop(
        0, tile, scan, (ends_ref[0], ends_ref[1], power[...]), unroll=4
    )
    ends_ref[0] = forward
    ends_ref[1] = backward
    power[...] = weight

    @pl.when(step == pl.num_programs(0) - 1)
    def _():
        for shard in range(all_ref.shape[0]):
            all_ref[shard] = ends_ref[...]


def modes(slabs, high, low, ratio, shards):
    count, levels, width = slabs[0].shape
    tile = min(TILE, count)
    total = high.shape[1]
    whole = lambda x: pl.BlockSpec(x.shape, lambda i: (0,) * x.ndim)
    return pl.pallas_call(
        modes_kernel,
        grid=(count // tile,),
        in_specs=[
            *[pl.BlockSpec((tile, levels, width), lambda i: (i, 0, 0))] * len(slabs),
            whole(high), whole(low), whole(ratio),
        ],
        out_specs=[
            pl.BlockSpec((tile, levels, total), lambda i: (i, 0, 0)),
            pl.BlockSpec((shards, 2, levels, total), lambda i: (0, 0, 0, 0)),
        ],
        out_shape=[
            jax.ShapeDtypeStruct((count, levels, total), f32),
            jax.ShapeDtypeStruct((shards, 2, levels, total), f32),
        ],
        scratch_shapes=[pltpu.VMEM((2, levels, total), f32), pltpu.VMEM((levels, total), f32)],
        compiler_params=params(),
        name="modes",
    )(*slabs, high, low, ratio)


def solve_kernel(
    place_ref, x_ref, ends_ref, ratio_ref, gain_ref, span_ref, high_ref, low_ref, prior_ref,
    *rest,
):
    outs, (all_ref, sum_ref, lines, tail, carry_ref, block) = rest[:-6], rest[-6:]
    step = pl.program_id(0)
    half = pl.num_programs(0) // 2
    shards = ends_ref.shape[0]
    tile, levels, total = x_ref.shape
    width = outs[0].shape[2]
    ratio = ratio_ref[...]

    @pl.when(step == 0)
    def _():
        span = span_ref[...]
        place = place_ref[0]
        weight = jnp.ones_like(span)
        forward = jnp.zeros_like(span)
        backward = jnp.zeros_like(span)
        for j in range(1, shards + 1):
            forward += weight * ends_ref[lax.rem(place - j + shards, shards), 0]
            backward += weight * ends_ref[lax.rem(place + j, shards), 1]
            weight = weight * span
        carry_ref[...] = forward / (1.0 - weight)
        tail[...] = backward / (1.0 - weight)
        sum_ref[...] = jnp.zeros_like(sum_ref)

    @pl.when(step < half)
    def _():
        def scan(a, y):
            y = x_ref[a] + ratio * y
            lines[step * tile + a] = y
            return y

        carry_ref[...] = lax.fori_loop(0, tile, scan, carry_ref[...], unroll=4)

    @pl.when(step == half)
    def _():
        carry_ref[...] = gain_ref[...] * (ratio * carry_ref[...] + tail[...])

    @pl.when(step >= half)
    def _():
        base = (2 * half - 1 - step) * tile

        def scan(j, carry):
            q, dot = carry
            a = tile - 1 - j
            q = ratio * (lines[base + a] + q)
            block[a] = q
            return q, dot + x_ref[a] * q

        zero = jnp.zeros((levels, total), f32)
        q, dot = lax.fori_loop(0, tile, scan, (carry_ref[...], zero), unroll=4)
        carry_ref[...] = q
        sum_ref[...] += dot
        back = product(block[...].reshape(tile * levels, total), high_ref, low_ref)
        for part, out in enumerate(outs):
            out[...] = back[:, part * width : (part + 1) * width].reshape(tile, levels, width)

    @pl.when(step == 2 * half - 1)
    def _():
        dots = fold(sum_ref[...])
        lanes = dots[:, :width]
        for start in range(width, total, width):
            lanes = lanes + dots[:, start : start + width]
        row = lax.broadcasted_iota(jnp.int32, (8, width), 0)
        sums = prior_ref[...] + jnp.where(row == 1, jnp.sum(lanes, axis=0, keepdims=True), 0.0)
        for device in range(all_ref.shape[0]):
            all_ref[device] = sums


def solve(place, x, ends, ratio, gain, span, high, low, prior, parts, copies):
    count, levels, total = x.shape
    tile = min(TILE, count)
    half = count // tile
    width = total // parts
    whole = lambda v: pl.BlockSpec(v.shape, lambda i, s: (0,) * v.ndim)
    back = lambda i: jnp.minimum(2 * half - 1 - i, half - 1)
    return pl.pallas_call(
        solve_kernel,
        grid_spec=pltpu.PrefetchScalarGridSpec(
            num_scalar_prefetch=1,
            grid=(2 * half,),
            in_specs=[
                pl.BlockSpec((tile, levels, total), lambda i, s: (jnp.minimum(i, 2 * half - 1 - i), 0, 0)),
                whole(ends), whole(ratio), whole(gain), whole(span), whole(high), whole(low), whole(prior),
            ],
            out_specs=[
                *[pl.BlockSpec((tile, levels, width), lambda i, s: (back(i), 0, 0))] * parts,
                pl.BlockSpec((copies, 8, width), lambda i, s: (0, 0, 0)),
            ],
            scratch_shapes=[
                pltpu.VMEM((levels, total), f32),
                pltpu.VMEM((count, levels, total), f32),
                pltpu.VMEM((levels, total), f32),
                pltpu.VMEM((levels, total), f32),
                pltpu.VMEM((tile, levels, total), f32),
            ],
        ),
        out_shape=[
            *[jax.ShapeDtypeStruct((count, levels, width), f32)] * parts,
            jax.ShapeDtypeStruct((copies, 8, width), f32),
        ],
        compiler_params=params(),
        name="solve",
    )(place, x, ends, ratio, gain, span, high, low, prior)


def scale_kernel(alpha_ref, in_ref, out_ref):
    out_ref[...] = (alpha_ref[0] * in_ref[...]).astype(bf16)


def scale_rows(alpha, moment):
    _, height, count, width = moment.shape
    return pl.pallas_call(
        scale_kernel,
        grid_spec=pltpu.PrefetchScalarGridSpec(
            num_scalar_prefetch=1,
            grid=(3 * height // 16,),
            in_specs=[pl.BlockSpec((1, 16, count, width), lambda i, s: (i // (height // 16), i % (height // 16), 0, 0))],
            out_specs=pl.BlockSpec((1, 16, count, width), lambda i, s: (i // (height // 16), i % (height // 16), 0, 0)),
        ),
        out_shape=jax.ShapeDtypeStruct((4, height, count, width), bf16),
        compiler_params=params(),
        name="scale_rows",
    )(alpha, moment)


def pressure_kernel(alpha_ref, *refs):
    pieces, (cos_ref, rest_ref, out_ref, rows) = refs[:-4], refs[-4:]
    tile, levels, width = pieces[0].shape
    height = levels * len(pieces)
    alpha = alpha_ref[0]

    def pair(j, carry):
        highs, lows = [], []
        for s in range(2):
            x = jnp.concatenate([piece[2 * j + s] for piece in pieces], axis=0)
            high, low = split(x)
            highs.append(high)
            lows.append(low)
        high = jnp.concatenate(highs, axis=1)
        low = jnp.concatenate(lows, axis=1)
        stacked = jnp.concatenate([high, low, high], axis=0)
        y = alpha * jnp.dot(cos_ref[...], stacked, preferred_element_type=f32)
        for s in range(2):
            rows[pl.ds(2 * j + s, height, stride=tile), :] = y[:, s * width : (s + 1) * width]
        return carry

    lax.fori_loop(0, tile // 2, pair, 0, unroll=4)
    for h in range(height):
        out_ref[0, h] = rows[h * tile : (h + 1) * tile, :].astype(bf16)


def pressure_rows(alpha, planes, cosine, rest):
    count, levels, width = planes[0].shape
    height = levels * len(planes)
    tile = min(TILE, count)
    high, low = split_table(cosine)
    table = jnp.concatenate([high, high, low], axis=1)
    return pl.pallas_call(
        pressure_kernel,
        grid_spec=pltpu.PrefetchScalarGridSpec(
            num_scalar_prefetch=1,
            grid=(count // tile,),
            in_specs=[
                *[pl.BlockSpec((tile, levels, width), lambda i, s: (i, 0, 0))] * len(planes),
                pl.BlockSpec(table.shape, lambda i, s: (0, 0)),
                pl.BlockSpec(memory_space=pl.ANY),
            ],
            out_specs=pl.BlockSpec((1, height, tile, width), lambda i, s: (3, 0, i, 0)),
            scratch_shapes=[pltpu.VMEM((height * tile, width), f32)],
        ),
        out_shape=jax.ShapeDtypeStruct(rest.shape, bf16),
        input_output_aliases={len(planes) + 2: 0},
        compiler_params=params(),
        name="pressure_rows",
    )(alpha, *planes, table, rest)


def cosine_table(extent):
    row_ids = jnp.arange(extent, dtype=f32)[:, None]
    col_ids = jnp.arange(extent, dtype=f32)[None, :]
    scaled = jnp.where(row_ids == 0, math.sqrt(1.0 / extent), math.sqrt(2.0 / extent))
    return scaled * jnp.cos(math.pi * (col_ids + 0.5) * row_ids / extent)


def pairwise(pieces, axis):
    count = lax.axis_size(axis)
    return [pieces[0]] + [
        lax.ppermute(pieces[s], axis, [(i, i ^ s) for i in range(count)]) for s in range(1, count)
    ]


def exchanged(copies, axis):
    return lax.all_to_all(copies, axis, split_axis=0, concat_axis=0, tiled=True)


def fence(*values):
    return lax.optimization_barrier(values)


def step(state, source, shear, permeability, radial_basis, radial_eigen):
    _, height, count, width = state.shape
    parts = lax.axis_size("rad")
    levels = height // parts // CHUNKS
    owner = lax.axis_index("rad") ^ jnp.arange(parts, dtype=jnp.int32)
    cosine = cosine_table(height).reshape(parts, CHUNKS, levels, height)
    cosine = jnp.swapaxes(jnp.take(cosine, owner, axis=0), 0, 1).reshape(height, height)

    cols_a = edges(state, permeability, 1, (0, 3))
    cols_b = edges(state, shear, 0, (1, 2))
    fluid_edges = neighbours(*cols_a)
    solid_edges = neighbours(*cols_b)
    *heights, fluid_rr = fluid(
        state, source, permeability, *fluid_edges, cosine, parts * CHUNKS
    )
    slabs = [pairwise(heights[c * parts : (c + 1) * parts], "rad") for c in range(CHUNKS)]
    basis = jnp.concatenate(pairwise([radial_basis] * parts, "rad"))
    high, low = split_table(basis)
    moment, rr, rz = momentum(state, shear, fluid_edges, solid_edges)
    *own, rr = fence(*[pieces[0] for pieces in slabs], rr)
    slabs = [[piece, *pieces[1:]] for piece, pieces in zip(own, slabs)]

    place = lax.axis_index("az").reshape(1)
    shards = lax.axis_size("az")
    sums = jnp.stack([jnp.sum(fluid_rr + rr, axis=0), jnp.sum(rz, axis=0)])
    sums = jnp.concatenate([sums, jnp.zeros((6, width), f32)])
    planes = []
    for chunk in range(CHUNKS):
        first = (lax.axis_index("rad") * CHUNKS + chunk) * levels
        level = (first + jnp.arange(levels, dtype=jnp.int32)).astype(f32)
        height_eigen = 4.0 * jnp.sin(math.pi * level / (2.0 * height)) ** 2
        center = storage + radial_eigen[None, :] + height_eigen[:, None]
        root = jnp.sqrt(center * (center + 4.0))
        ratio = 2.0 / (center + 2.0 + root)
        span = lax.integer_pow(ratio, count)
        x, ends = modes(slabs[chunk], high, low, ratio, shards)
        ends = exchanged(ends, "az")
        last = chunk == CHUNKS - 1
        copies = shards * parts if last else 1
        *back, sums = solve(
            place, x, ends, ratio, 1.0 / root, span, high.T, low.T, sums, parts, copies
        )
        if last:
            sums = exchanged(sums, ("az", "rad"))
        else:
            sums = sums[0]
        planes += pairwise(back, "rad")
    totals = jnp.sum(sums, axis=(0, 2))
    alpha = (totals[0] / totals[1]).reshape(1)
    out = scale_rows(alpha, moment)
    return pressure_rows(alpha, planes, cosine.T, out)


def solution(mesh):
    placed = (
        P(None, None, "az", "rad"),
        P(None, "az", "rad"),
        P(None, "az", "rad"),
        P(None, "az", "rad"),
        P("rad", None),
        P(),
    )
    return jax.shard_map(
        step, mesh=mesh, in_specs=placed, out_specs=P(None, None, "az", "rad"), check_vma=False
    )
```

```python
import functools
import math

import jax
import jax.numpy as jnp
from jax import lax
from jax.experimental import pallas as pl
from jax.experimental.pallas import tpu as pltpu
from jax.sharding import PartitionSpec as P


biot_coupling = 2.0
storage = 1.0

f32 = jnp.float32
bf16 = jnp.bfloat16


SLAB = 8
EDGE = 16
ROWS = 32
TILE = 64
HALVES = 2
CHUNKS = 2


def params(limit=56):
    return pltpu.CompilerParams(
        dimension_semantics=("arbitrary",), vmem_limit_bytes=limit * 1024 * 1024
    )


def lanes_of(shape):
    return lax.broadcasted_iota(jnp.int32, shape, len(shape) - 1)


def split(x):
    high = x.astype(bf16)
    low = (x - high.astype(f32)).astype(bf16)
    return high, low


def fold(x):
    total = x[0:8]
    for start in range(8, x.shape[0], 8):
        total = total + x[start : start + 8]
    return total


def split_table(x):
    rounded = lax.reduce_precision(x, exponent_bits=8, mantissa_bits=7)
    return rounded.astype(bf16), (x - rounded).astype(bf16)


def edges_kernel(state_ref, shear_ref, perm_ref, cols_ref, *rest):
    *row_refs, acc = rest
    step = pl.program_id(0)
    slab, count, width = shear_ref.shape
    rows = min(64, count // 2)
    places = (0, count // 2 - 1, count // 2, count - 1)
    lane = lanes_of((rows, width))
    for c in range(6):
        src = state_ref.at[c] if c < 4 else (shear_ref, perm_ref)[c - 4]
        for start in range(0, count, rows):
            value = acc[c, start : start + rows, :]
            for i in range(slab):
                h = step * slab + i
                x = src[i, start : start + rows, :].astype(f32)
                value = jnp.where((lane >> 1) == h, pltpu.roll(x, 2 * h + 1, 1), value)
                for place, row_ref in zip(places, row_refs):
                    if start <= place < start + rows:
                        row_ref[c, pl.ds(h, 1), :] = x[place - start : place - start + 1]
            acc[c, start : start + rows, :] = value

    @pl.when(step == pl.num_programs(0) - 1)
    def _():
        for c in range(6):
            for start in range(0, count, rows):
                v = acc[c, start : start + rows, :]
                swapped = jnp.where(lane % 2 == 0, pltpu.roll(v, width - 1, 1), pltpu.roll(v, 1, 1))
                cols_ref[c, start : start + rows, :] = swapped.astype(bf16)


def edges(state, shear, perm):
    _, height, count, width = state.shape
    whole = lambda *shape: pl.BlockSpec(shape, lambda i: (0,) * len(shape))
    return pl.pallas_call(
        edges_kernel,
        grid=(height // EDGE,),
        in_specs=[
            pl.BlockSpec((4, EDGE, count, width), lambda i: (0, i, 0, 0)),
            pl.BlockSpec((EDGE, count, width), lambda i: (i, 0, 0)),
            pl.BlockSpec((EDGE, count, width), lambda i: (i, 0, 0)),
        ],
        out_specs=[whole(6, count, width), *[whole(6, height, width)] * 4],
        out_shape=[
            jax.ShapeDtypeStruct((6, count, width), bf16),
            *[jax.ShapeDtypeStruct((6, height, width), f32)] * 4,
        ],
        scratch_shapes=[pltpu.VMEM((6, count, width), f32)],
        compiler_params=params(),
        name="edges",
    )(state, shear, perm)


def neighbours(cols, first, low, high, last):
    n_rad = lax.axis_size("rad")
    n_az = lax.axis_size("az")
    from_right = lax.ppermute(cols, "rad", [(i + 1, i) for i in range(n_rad - 1)])
    from_left = lax.ppermute(cols, "rad", [(i, i + 1) for i in range(n_rad - 1)])
    before = lax.ppermute(last, "az", [(i, (i + 1) % n_az) for i in range(n_az)])
    after = lax.ppermute(first, "az", [((i + 1) % n_az, i) for i in range(n_az)])
    beside = jnp.where(lanes_of(cols.shape) % 2 == 0, from_right, from_left)
    return beside, before, after, low, high


def stage(scratch, center, above, below, before, after, step, steps, slab, count):
    top = jnp.where(step > 0, 1.0, 0.0)
    bottom = jnp.where(step < steps - 1, 1.0, 0.0)
    scratch[0, 8 : 8 + count, :] = above[...].astype(f32) * top
    scratch[slab + 1, 8 : 8 + count, :] = below[...].astype(f32) * bottom
    for i in range(slab):
        scratch[i + 1, 8 : 8 + count, :] = center[i].astype(f32)
        if before is not None:
            h = step * slab + i
            scratch[i + 1, 7:8, :] = before[pl.ds(h, 1), :]
            scratch[i + 1, 8 + count : 9 + count, :] = after[pl.ds(h, 1), :]


def radial_pair(x, beside, shift, lane):
    width = x.shape[1]
    beside = pltpu.roll(beside, shift, 1)
    right = jnp.where(lane == width - 1, beside, pltpu.roll(x, width - 1, 1))
    left = jnp.where(lane == 0, beside, pltpu.roll(x, 1, 1))
    return right.astype(f32), left.astype(f32)


def weighted(center, faces, around):
    total = faces[1][0] * around[0]
    for face, other in zip(faces[1][1:], around[1:]):
        total = total + face * other
    return faces[0] * center - total


def total_of(values):
    total = values[0]
    for value in values[1:]:
        total = total + value
    return total


def fluid_kernel(
    shared, p_ref, p_up, p_dn, k_ref, k_up, k_dn, z_ref, z_up, z_dn, r_ref, t_ref, src_ref,
    beside_ref, before_ref, after_ref, cos_ref,
    *rest,
):
    outs, (sum_ref, ps, ks, zs, ts, res) = rest[shared:-6], rest[-6:]
    step = pl.program_id(0)
    slab, count, width = src_ref.shape
    height = before_ref.shape[1]
    steps = height // slab
    tile, levels, _ = outs[0].shape

    @pl.when(step == 0)
    def _():
        sum_ref[...] = jnp.zeros_like(sum_ref)

    @pl.when(step < steps)
    def _():
        stage(ps, p_ref.at[0], p_up.at[0, 0], p_dn.at[0, 0], before_ref.at[3], after_ref.at[3], step, steps, slab, count)
        stage(ks, k_ref, k_up.at[0], k_dn.at[0], before_ref.at[5], after_ref.at[5], step, steps, slab, count)
        stage(zs, z_ref.at[0], z_up.at[0, 0], z_dn.at[0, 0], None, None, step, steps, slab, count)
        for i in range(slab):
            h = step * slab + i
            ts[i, 8 : 8 + count, :] = t_ref[0, i].astype(f32)
            ts[i, 7:8, :] = before_ref[1, pl.ds(h, 1), :]
            ts[i, 8 + count : 9 + count, :] = after_ref[1, pl.ds(h, 1), :]
        lane = lanes_of((ROWS, width))

        def plane(i, total):
            h = step * slab + i
            shift = 2 * height - 1 - 2 * h
            for a in range(0, count, ROWS):
                at = slice(8 + a, 8 + a + ROWS)
                prev = slice(7 + a, 7 + a + ROWS)
                nxt = slice(9 + a, 9 + a + ROWS)
                own = slice(a, a + ROWS)
                p = ps[i + 1, at, :]
                k = ks[i + 1, at, :]
                p_r, p_l = radial_pair(p_ref[0, i, own, :], beside_ref[3, own, :], shift, lane)
                k_r, k_l = radial_pair(k_ref[i, own, :], beside_ref[5, own, :], shift, lane)
                others = [ks[i + 1, nxt, :], ks[i + 1, prev, :], ks[i + 2, at, :], ks[i, at, :]]
                faces = [k + other for other in (k_r, k_l, *others)]
                around = [ps[i + 1, nxt, :], ps[i + 1, prev, :], ps[i + 2, at, :], ps[i, at, :]]
                flux = weighted(p, (total_of(faces), faces), (p_r, p_l, *around))
                u_r, u_l = radial_pair(r_ref[0, i, own, :], beside_ref[0, own, :], shift, lane)
                spread = (u_r - u_l) + (ts[i, nxt, :] - ts[i, prev, :])
                spread += zs[i + 2, at, :] - zs[i, at, :]
                if biot_coupling != 2.0:
                    spread = (0.5 * biot_coupling) * spread
                value = (src_ref[i, own, :].astype(f32) + spread) + (storage * p + 0.5 * flux)
                res[h, own, :] = value
                total = total + fold(value * value)
            return total

        sum_ref[...] += lax.fori_loop(0, slab, plane, jnp.zeros((8, width), f32))

    @pl.when(step >= steps)
    def _():
        base = (step - steps) * tile

        def group(j, carry):
            start = pl.multiple_of(base + 8 * j, 8)
            columns = [
                jnp.swapaxes(res[h : h + 8, pl.ds(start, 8), :], 0, 1) for h in range(0, height, 8)
            ]
            for pair in range(4):
                highs, lows = [], []
                for s in range(2):
                    x = jnp.concatenate([column[2 * pair + s] for column in columns], axis=0)
                    high, low = split(x)
                    highs.append(high)
                    lows.append(low)
                high = jnp.concatenate(highs, axis=1)
                low = jnp.concatenate(lows, axis=1)
                stacked = jnp.concatenate([high, low, high], axis=0)
                y = jnp.dot(cos_ref[...], stacked, preferred_element_type=f32)
                for s in range(2):
                    for block, out in enumerate(outs):
                        out[8 * j + 2 * pair + s, :, :] = y[
                            block * levels : (block + 1) * levels, s * width : (s + 1) * width
                        ]
            return carry

        lax.fori_loop(0, tile // 8, group, 0)


def plane_specs(channel, slab, steps, count, width, base=0, part=0):
    at = lambda i: jnp.minimum(i + base, steps - 1)
    up = lambda i: jnp.maximum(at(i) * slab - 1, 0)
    down = lambda i: jnp.minimum(at(i) * slab + slab, steps * slab - 1)
    if channel is None:
        return [
            pl.BlockSpec((slab, count, width), lambda i: (at(i), part, 0)),
            pl.BlockSpec((1, count, width), lambda i: (up(i), part, 0)),
            pl.BlockSpec((1, count, width), lambda i: (down(i), part, 0)),
        ]
    return [
        pl.BlockSpec((1, slab, count, width), lambda i: (channel, at(i), part, 0)),
        pl.BlockSpec((1, 1, count, width), lambda i: (channel, up(i), part, 0)),
        pl.BlockSpec((1, 1, count, width), lambda i: (channel, down(i), part, 0)),
    ]


def fluid(state, source, perm, beside, before, after, table, parts, half, shared):
    _, height, whole_count, width = state.shape
    count = whole_count // HALVES
    steps = height // SLAB
    tile = min(TILE, count)
    pieces = parts * CHUNKS
    levels = height // pieces
    specs = lambda c: plane_specs(c, SLAB, steps, count, width, part=half)
    whole = lambda x: pl.BlockSpec(x.shape, lambda i: (0,) * x.ndim)
    at = lambda first: pl.BlockSpec(
        (tile, levels, width), lambda i: (first + jnp.maximum(i - steps, 0), 0, 0)
    )
    rest = pieces - parts
    return pl.pallas_call(
        functools.partial(fluid_kernel, len(shared)),
        grid=(steps + count // tile,),
        in_specs=[
            *specs(3), *specs(None), *specs(2), specs(0)[0], specs(1)[0], specs(None)[0],
            pl.BlockSpec((6, count, width), lambda i: (0, half, 0)), whole(before), whole(after), whole(table),
            *[pl.BlockSpec(memory_space=pl.ANY)] * len(shared),
        ],
        out_specs=[
            *[at(0)] * parts, *[at(half * (count // tile))] * rest,
            pl.BlockSpec((8, width), lambda i: (0, 0)),
        ],
        out_shape=[
            *[jax.ShapeDtypeStruct((count, levels, width), f32)] * parts,
            *[jax.ShapeDtypeStruct((whole_count, levels, width), f32)] * rest,
            jax.ShapeDtypeStruct((8, width), f32),
        ],
        scratch_shapes=[
            pltpu.VMEM((SLAB + 2, count + 16, width), f32),
            pltpu.VMEM((SLAB + 2, count + 16, width), f32),
            pltpu.VMEM((SLAB + 2, count + 16, width), f32),
            pltpu.VMEM((SLAB, count + 16, width), f32),
            pltpu.VMEM((height, count, width), f32),
        ],
        input_output_aliases={16 + i: pieces - len(shared) + i for i in range(len(shared))},
        compiler_params=params(),
        name="fluid",
    )(state, state, state, perm, perm, perm, state, state, state, state, state, source,
      beside, before, after, table, *shared)


def momentum_kernel(base, steps, priors, *refs):
    fields = [refs[3 * c : 3 * c + 3] for c in range(5)]
    beside_ref, before_ref, after_ref = refs[15:18]
    prior_refs = refs[18 : 18 + priors]
    *_, out_ref, rr_ref, rz_ref = refs[:-5]
    scratch = refs[-5:]
    step = pl.program_id(0) + base
    _, slab, count, width = out_ref.shape
    height = before_ref.shape[1]

    @pl.when(step == base)
    def _():
        rr_ref[...] = total_of([prior[...] for prior in prior_refs[::2]])
        rz_ref[...] = total_of([prior[...] for prior in prior_refs[1::2]])

    for c in range(5):
        center, up, down = fields[c]
        if c < 4:
            center, up, down = center.at[0], up.at[0, 0], down.at[0, 0]
        else:
            up, down = up.at[0], down.at[0]
        stage(scratch[c], center, up, down, before_ref.at[c], after_ref.at[c], step, steps, slab, count)
    lane = lanes_of((ROWS, width))

    def plane(i, totals):
        rr, rz = totals
        h = step * slab + i
        shift = 2 * height - 1 - 2 * h
        for a in range(0, count, ROWS):
            at = slice(8 + a, 8 + a + ROWS)
            prev = slice(7 + a, 7 + a + ROWS)
            nxt = slice(9 + a, 9 + a + ROWS)
            own = slice(a, a + ROWS)

            def around(c):
                s = scratch[c]
                center = fields[c][0].at[0] if c < 4 else fields[c][0]
                right, left = radial_pair(center[i, own, :], beside_ref[c, own, :], shift, lane)
                others = [s[i + 1, nxt, :], s[i + 1, prev, :], s[i + 2, at, :], s[i, at, :]]
                return s[i + 1, at, :], (right, left, *others)

            g, g_around = around(4)
            faces = [g + other for other in g_around]
            diagonal = total_of(faces)
            inverse = -1.0 / diagonal
            _, p = around(3)
            squares = None
            for c in range(3):
                u, u_around = around(c)
                value = weighted(u, (diagonal, faces), u_around)
                value = value + biot_coupling * (p[2 * c] - p[2 * c + 1])
                out_ref[c, i, own, :] = value * inverse
                squares = value * value if squares is None else squares + value * value
            rr = rr + fold(squares)
            rz = rz + fold(squares * inverse)
        return rr, rz

    zero = jnp.zeros((8, width), f32)
    rr, rz = lax.fori_loop(0, slab, plane, (zero, zero))
    rr_ref[...] += 0.25 * rr
    rz_ref[...] -= 0.5 * rz


def momentum(state, shear, beside, before, after, piece, prior, rows=None):
    _, height, count, width = state.shape
    steps = height // SLAB
    base, end = ((eighth * steps) // 8 for eighth in piece)
    specs = lambda c: plane_specs(c, SLAB, steps, count, width, base=base)
    whole = lambda x: pl.BlockSpec(x.shape, lambda i: (0,) * x.ndim)
    operands = [*[state] * 12, shear, shear, shear, beside, before, after, *prior]
    in_specs = [
        *specs(0), *specs(1), *specs(2), *specs(3), *specs(None),
        *[whole(x) for x in operands[15:]],
    ]
    aliases = {}
    if rows is not None:
        aliases = {len(operands): 0}
        operands.append(rows)
        in_specs.append(pl.BlockSpec(memory_space=pl.ANY))
    return pl.pallas_call(
        functools.partial(momentum_kernel, base, steps, len(prior)),
        grid=(end - base,),
        in_specs=in_specs,
        out_specs=[
            pl.BlockSpec((3, SLAB, count, width), lambda i: (0, i + base, 0, 0)),
            pl.BlockSpec((8, width), lambda i: (0, 0)),
            pl.BlockSpec((8, width), lambda i: (0, 0)),
        ],
        out_shape=[
            jax.ShapeDtypeStruct((3, height, count, width), f32),
            jax.ShapeDtypeStruct((8, width), f32),
            jax.ShapeDtypeStruct((8, width), f32),
        ],
        scratch_shapes=[pltpu.VMEM((SLAB + 2, count + 16, width), f32)] * 5,
        input_output_aliases=aliases,
        compiler_params=params(),
        name="momentum",
    )(*operands)


def product(x, high_ref, low_ref):
    high, low = split(x)
    y = jnp.dot(high, high_ref[...], preferred_element_type=f32)
    y = y + jnp.dot(low, high_ref[...], preferred_element_type=f32)
    return y + jnp.dot(high, low_ref[...], preferred_element_type=f32)


def modes_kernel(groups, *refs):
    slabs, (high_ref, low_ref, ratio_ref, x_ref, all_ref, ends_ref, power) = refs[:-7], refs[-7:]
    step = pl.program_id(0)
    tile, levels, width = slabs[0].shape

    @pl.when(step == 0)
    def _():
        ends_ref[...] = jnp.zeros_like(ends_ref)
        power[...] = jnp.ones_like(power)

    each = len(slabs) // groups
    span = pl.num_programs(0) // groups
    for half in range(groups):

        @pl.when((step >= half * span) & (step < (half + 1) * span))
        def _():
            mine = slabs[half * each : (half + 1) * each]
            lines = jnp.concatenate([slab[...].reshape(tile * levels, width) for slab in mine], axis=1)
            x_ref[...] = product(lines, high_ref, low_ref).reshape(x_ref.shape)

    ratio = ratio_ref[...]

    def scan(a, carry):
        forward, backward, weight = carry
        x = x_ref[a]
        return x + ratio * forward, backward + weight * x, weight * ratio

    forward, backward, weight = lax.fori_loop(
        0, tile, scan, (ends_ref[0], ends_ref[1], power[...]), unroll=4
    )
    ends_ref[0] = forward
    ends_ref[1] = backward
    power[...] = weight

    @pl.when(step == pl.num_programs(0) - 1)
    def _():
        for shard in range(all_ref.shape[0]):
            all_ref[shard] = ends_ref[...]


def modes(groups, high, low, ratio, shards):
    slabs = sum(groups, [])
    span, levels, width = slabs[0].shape
    count = span * len(groups)
    tile = min(TILE, span)
    total = high.shape[1]
    steps = span // tile
    at = lambda half: pl.BlockSpec(
        (tile, levels, width), lambda i: (jnp.clip(i - half * steps, 0, steps - 1), 0, 0)
    )
    whole = lambda x: pl.BlockSpec(x.shape, lambda i: (0,) * x.ndim)
    return pl.pallas_call(
        functools.partial(modes_kernel, len(groups)),
        grid=(count // tile,),
        in_specs=[
            *[at(half) for half, group in enumerate(groups) for _ in group],
            whole(high), whole(low), whole(ratio),
        ],
        out_specs=[
            pl.BlockSpec((tile, levels, total), lambda i: (i, 0, 0)),
            pl.BlockSpec((shards, 2, levels, total), lambda i: (0, 0, 0, 0)),
        ],
        out_shape=[
            jax.ShapeDtypeStruct((count, levels, total), f32),
            jax.ShapeDtypeStruct((shards, 2, levels, total), f32),
        ],
        scratch_shapes=[pltpu.VMEM((2, levels, total), f32), pltpu.VMEM((levels, total), f32)],
        compiler_params=params(),
        name="modes",
    )(*slabs, high, low, ratio)


def solve_kernel(
    last, place_ref, x_ref, ends_ref, ratio_ref, gain_ref, span_ref, high_ref, low_ref,
    rr_ref, rz_ref, prior_ref, *rest,
):
    outs, (all_ref, sum_ref, lines, tail, carry_ref, block) = rest[:-6], rest[-6:]
    step = pl.program_id(0)
    half = pl.num_programs(0) // 2
    shards = ends_ref.shape[0]
    tile, levels, total = x_ref.shape
    width = outs[0].shape[2]
    ratio = ratio_ref[...]

    @pl.when(step == 0)
    def _():
        span = span_ref[...]
        place = place_ref[0]
        weight = jnp.ones_like(span)
        forward = jnp.zeros_like(span)
        backward = jnp.zeros_like(span)
        for j in range(1, shards + 1):
            forward += weight * ends_ref[lax.rem(place - j + shards, shards), 0]
            backward += weight * ends_ref[lax.rem(place + j, shards), 1]
            weight = weight * span
        carry_ref[...] = forward / (1.0 - weight)
        tail[...] = backward / (1.0 - weight)
        sum_ref[...] = jnp.zeros_like(sum_ref)

    @pl.when(step < half)
    def _():
        def scan(a, y):
            y = x_ref[a] + ratio * y
            lines[step * tile + a] = y
            return y

        carry_ref[...] = lax.fori_loop(0, tile, scan, carry_ref[...], unroll=4)

    @pl.when(step == half)
    def _():
        carry_ref[...] = gain_ref[...] * (ratio * carry_ref[...] + tail[...])

    @pl.when(step >= half)
    def _():
        base = (2 * half - 1 - step) * tile

        def scan(j, carry):
            q, dot = carry
            a = tile - 1 - j
            q = ratio * (lines[base + a] + q)
            block[a] = q
            return q, dot + x_ref[a] * q

        zero = jnp.zeros((levels, total), f32)
        q, dot = lax.fori_loop(0, tile, scan, (carry_ref[...], zero), unroll=4)
        carry_ref[...] = q
        sum_ref[...] += dot
        back = product(block[...].reshape(tile * levels, total), high_ref, low_ref)
        for part, out in enumerate(outs):
            out[...] = back[:, part * width : (part + 1) * width].reshape(tile, levels, width)

    @pl.when(step == 2 * half - 1)
    def _():
        dots = fold(sum_ref[...])
        lanes = dots[:, :width]
        for start in range(width, total, width):
            lanes = lanes + dots[:, start : start + width]
        sums = lanes + prior_ref[...]
        if last:
            row = lax.broadcasted_iota(jnp.int32, (8, width), 0)
            rr = jnp.sum(rr_ref[...], axis=0, keepdims=True)
            rz = jnp.sum(rz_ref[...] + sums, axis=0, keepdims=True)
            sums = jnp.where(row == 0, rr, jnp.where(row == 1, rz, 0.0))
        for device in range(all_ref.shape[0]):
            all_ref[device] = sums


def solve(place, x, ends, ratio, gain, span, high, low, rr, rz, prior, parts, copies, last):
    count, levels, total = x.shape
    tile = min(TILE, count)
    half = count // tile
    width = total // parts
    whole = lambda v: pl.BlockSpec(v.shape, lambda i, s: (0,) * v.ndim)
    back = lambda i: jnp.minimum(2 * half - 1 - i, half - 1)
    return pl.pallas_call(
        functools.partial(solve_kernel, last),
        grid_spec=pltpu.PrefetchScalarGridSpec(
            num_scalar_prefetch=1,
            grid=(2 * half,),
            in_specs=[
                pl.BlockSpec((tile, levels, total), lambda i, s: (jnp.minimum(i, 2 * half - 1 - i), 0, 0)),
                whole(ends), whole(ratio), whole(gain), whole(span), whole(high), whole(low), whole(rr), whole(rz), whole(prior),
            ],
            out_specs=[
                *[pl.BlockSpec((tile, levels, width), lambda i, s: (back(i), 0, 0))] * parts,
                pl.BlockSpec((copies, 8, width), lambda i, s: (0, 0, 0)),
            ],
            scratch_shapes=[
                pltpu.VMEM((levels, total), f32),
                pltpu.VMEM((count, levels, total), f32),
                pltpu.VMEM((levels, total), f32),
                pltpu.VMEM((levels, total), f32),
                pltpu.VMEM((tile, levels, total), f32),
            ],
        ),
        out_shape=[
            *[jax.ShapeDtypeStruct((count, levels, width), f32)] * parts,
            jax.ShapeDtypeStruct((copies, 8, width), f32),
        ],
        compiler_params=params(),
        name="solve",
    )(place, x, ends, ratio, gain, span, high, low, rr, rz, prior)


def scale_kernel(alpha_ref, in_ref, out_ref):
    out_ref[...] = (alpha_ref[0] * in_ref[...]).astype(bf16)


def scale_rows(alpha, moment):
    _, height, count, width = moment.shape
    return pl.pallas_call(
        scale_kernel,
        grid_spec=pltpu.PrefetchScalarGridSpec(
            num_scalar_prefetch=1,
            grid=(3 * height // 16,),
            in_specs=[pl.BlockSpec((1, 16, count, width), lambda i, s: (i // (height // 16), i % (height // 16), 0, 0))],
            out_specs=pl.BlockSpec((1, 16, count, width), lambda i, s: (i // (height // 16), i % (height // 16), 0, 0)),
        ),
        out_shape=jax.ShapeDtypeStruct((4, height, count, width), bf16),
        compiler_params=params(),
        name="scale_rows",
    )(alpha, moment)


def pressure_kernel(alpha_ref, *refs):
    pieces, (cos_ref, rest_ref, out_ref) = refs[:-3], refs[-3:]
    tile, levels, width = pieces[0].shape
    height = levels * len(pieces)
    alpha = alpha_ref[0]

    def group(j, carry):
        planes = []
        for pair in range(8):
            highs, lows = [], []
            for s in range(2):
                a = 16 * j + 2 * pair + s
                x = jnp.concatenate([piece[a] for piece in pieces], axis=0)
                high, low = split(x)
                highs.append(high)
                lows.append(low)
            high = jnp.concatenate(highs, axis=1)
            low = jnp.concatenate(lows, axis=1)
            stacked = jnp.concatenate([high, low, high], axis=0)
            y = alpha * jnp.dot(cos_ref[...], stacked, preferred_element_type=f32)
            planes += [y[:, :width], y[:, width:]]
        start = pl.multiple_of(16 * j, 16)
        for h in range(0, height, 8):
            low = jnp.swapaxes(jnp.stack([y[h : h + 8] for y in planes[:8]]), 0, 1)
            high = jnp.swapaxes(jnp.stack([y[h : h + 8] for y in planes[8:]]), 0, 1)
            block = jnp.concatenate([low, high], axis=1)
            out_ref[0, h : h + 8, pl.ds(start, 16), :] = block.astype(bf16)
        return carry

    lax.fori_loop(0, tile // 16, group, 0)


def pressure_rows(alpha, planes, cosine, rest):
    count, levels, width = planes[0].shape
    height = levels * len(planes)
    tile = min(TILE, count)
    high, low = split_table(cosine)
    table = jnp.concatenate([high, high, low], axis=1)
    return pl.pallas_call(
        pressure_kernel,
        grid_spec=pltpu.PrefetchScalarGridSpec(
            num_scalar_prefetch=1,
            grid=(count // tile,),
            in_specs=[
                *[pl.BlockSpec((tile, levels, width), lambda i, s: (i, 0, 0))] * len(planes),
                pl.BlockSpec(table.shape, lambda i, s: (0, 0)),
                pl.BlockSpec(memory_space=pl.ANY),
            ],
            out_specs=pl.BlockSpec((1, height, tile, width), lambda i, s: (3, 0, i, 0)),
        ),
        out_shape=jax.ShapeDtypeStruct(rest.shape, bf16),
        input_output_aliases={len(planes) + 2: 0},
        compiler_params=params(),
        name="pressure_rows",
    )(alpha, *planes, table, rest)


def cosine_table(extent):
    row_ids = jnp.arange(extent, dtype=f32)[:, None]
    col_ids = jnp.arange(extent, dtype=f32)[None, :]
    scaled = jnp.where(row_ids == 0, math.sqrt(1.0 / extent), math.sqrt(2.0 / extent))
    return scaled * jnp.cos(math.pi * (col_ids + 0.5) * row_ids / extent)


def pairwise(pieces, axis):
    count = lax.axis_size(axis)
    return [pieces[0]] + [
        lax.ppermute(pieces[s], axis, [(i, i ^ s) for i in range(count)]) for s in range(1, count)
    ]


def exchanged(copies, axis):
    return lax.all_to_all(copies, axis, split_axis=0, concat_axis=0, tiled=True)


def fence(*values):
    return lax.optimization_barrier(values)


def step(state, source, shear, permeability, radial_basis, radial_eigen):
    _, height, count, width = state.shape
    parts = lax.axis_size("rad")
    levels = height // parts // CHUNKS
    owner = lax.axis_index("rad") ^ jnp.arange(parts, dtype=jnp.int32)
    cosine = cosine_table(height).reshape(parts, CHUNKS, levels, height)
    cosine = jnp.swapaxes(jnp.take(cosine, owner, axis=0), 0, 1).reshape(height, height)
    high, low = split_table(cosine)
    table = jnp.concatenate([high, high, low], axis=1)

    cols, first, *others = edges(state, shear, permeability)
    first, radial_basis = fence(first, radial_basis)
    beside, before, after, mid_low, mid_high = neighbours(cols, first, *others)
    blocks = pairwise([radial_basis] * parts, "rad")
    sent, priors, shared = [], [], []
    for half, ends in enumerate(((before, mid_high), (mid_low, after))):
        *heights, fluid_rr = fluid(
            state, source, permeability, beside, *ends, table, parts, half, shared
        )
        shared = heights[parts:]
        sent.append(pairwise(heights[:parts], "rad"))
        priors += [fluid_rr, jnp.zeros_like(fluid_rr)]
    slabs = [sent]
    for chunk in range(1, CHUNKS):
        slabs.append([pairwise(shared[(chunk - 1) * parts : chunk * parts], "rad")])
    high, low = split_table(jnp.concatenate(blocks))
    around = (beside, before, after)
    moment, rr, rz = momentum(state, shear, *around, (0, 2), priors)

    place = lax.axis_index("az").reshape(1)
    shards = lax.axis_size("az")
    sums = jnp.zeros((8, width), f32)
    planes = []
    for chunk in range(CHUNKS):
        first = (lax.axis_index("rad") * CHUNKS + chunk) * levels
        level = (first + jnp.arange(levels, dtype=jnp.int32)).astype(f32)
        height_eigen = 4.0 * jnp.sin(math.pi * level / (2.0 * height)) ** 2
        center = storage + radial_eigen[None, :] + height_eigen[:, None]
        root = jnp.sqrt(center * (center + 4.0))
        ratio = 2.0 / (center + 2.0 + root)
        span = lax.integer_pow(ratio, count)
        x, ends = modes(slabs[chunk], high, low, ratio, shards)
        ends = exchanged(ends, "az")
        piece = ((2, 3), (6, 8))[chunk]
        moment, rr, rz = momentum(state, shear, *around, piece, (rr, rz), moment)
        last = chunk == CHUNKS - 1
        copies = shards * parts if last else 1
        *back, sums = solve(
            place, x, ends, ratio, 1.0 / root, span, high.T, low.T, rr, rz, sums, parts, copies, last
        )
        if last:
            sums = exchanged(sums, ("az", "rad"))
        else:
            sums = sums[0]
            moment, rr, rz = momentum(state, shear, *around, (3, 6), (rr, rz), moment)
        planes += pairwise(back, "rad")
    totals = jnp.sum(sums, axis=(0, 2))
    alpha = (totals[0] / totals[1]).reshape(1)
    out = scale_rows(alpha, moment)
    return pressure_rows(alpha, planes, cosine.T, out)


def solution(mesh):
    placed = (
        P(None, None, "az", "rad"),
        P(None, "az", "rad"),
        P(None, "az", "rad"),
        P(None, "az", "rad"),
        P("rad", None),
        P(),
    )
    return jax.shard_map(
        step, mesh=mesh, in_specs=placed, out_specs=P(None, None, "az", "rad"), check_vma=False
    )
```

```python
import functools
import math

import jax
import jax.numpy as jnp
from jax import lax
from jax.experimental import pallas as pl
from jax.experimental.pallas import tpu as pltpu
from jax.sharding import PartitionSpec as P


biot_coupling = 2.0
storage = 1.0

f32 = jnp.float32
bf16 = jnp.bfloat16


SLAB = 8
FLUID = 16
PICKED = (1, 2, 4)
EDGE = 16
ROWS = 32
TILE = 64
HALVES = 2
CHUNKS = 2


def params(limit=56):
    return pltpu.CompilerParams(
        dimension_semantics=("arbitrary",), vmem_limit_bytes=limit * 1024 * 1024
    )


def lanes_of(shape):
    return lax.broadcasted_iota(jnp.int32, shape, len(shape) - 1)


def split(x):
    high = x.astype(bf16)
    low = (x - high.astype(f32)).astype(bf16)
    return high, low


def fold(x):
    total = x[0:8]
    for start in range(8, x.shape[0], 8):
        total = total + x[start : start + 8]
    return total


def split_table(x):
    rounded = lax.reduce_precision(x, exponent_bits=8, mantissa_bits=7)
    return rounded.astype(bf16), (x - rounded).astype(bf16)


def edges_kernel(state_ref, shear_ref, perm_ref, cols_ref, *rest):
    *row_refs, acc, chosen = rest
    step = pl.program_id(0)
    slab, count, width = shear_ref.shape
    rows = min(64, count // 2)
    places = (0, count // 2 - 1, count // 2, count - 1)
    lane = lanes_of((rows, width))
    sources = [state_ref.at[c] if c < 4 else (shear_ref, perm_ref)[c - 4] for c in range(6)]

    @pl.when(step == 0)
    def _():
        row = lax.broadcasted_iota(jnp.int32, (slab * width, width), 0)
        plane = lax.div(row, width)
        spot = lax.rem(row, width)
        column = lanes_of((slab * width, width))
        wanted = (spot == 0) & (column == 2 * plane + 1) | (spot == width - 1) & (column == 2 * plane)
        chosen[...] = jnp.where(wanted, 1.0, 0.0).astype(bf16)
        for c in PICKED:
            acc[c] = jnp.zeros_like(acc[c])

    for c in PICKED:
        src = sources[c]
        planes = jnp.concatenate([src[i] for i in range(slab)], axis=1)
        packed = jnp.dot(planes, chosen[...], preferred_element_type=f32)
        acc[c] += pltpu.roll(packed, 2 * slab * step, 1)
        for i in range(slab):
            h = step * slab + i
            for place, row_ref in zip(places, row_refs):
                start = place // 16 * 16
                x = src[i, start : start + 16, :].astype(f32)
                row_ref[c, pl.ds(h, 1), :] = x[place - start : place - start + 1]

    for c in range(6):
        if c in PICKED:
            continue
        src = sources[c]
        for start in range(0, count, rows):
            value = acc[c, start : start + rows, :]
            for i in range(slab):
                h = step * slab + i
                x = src[i, start : start + rows, :].astype(f32)
                value = jnp.where((lane >> 1) == h, pltpu.roll(x, 2 * h + 1, 1), value)
                for place, row_ref in zip(places, row_refs):
                    if start <= place < start + rows:
                        row_ref[c, pl.ds(h, 1), :] = x[place - start : place - start + 1]
            acc[c, start : start + rows, :] = value

    @pl.when(step == pl.num_programs(0) - 1)
    def _():
        for c in range(6):
            for start in range(0, count, rows):
                v = acc[c, start : start + rows, :]
                swapped = jnp.where(lane % 2 == 0, pltpu.roll(v, width - 1, 1), pltpu.roll(v, 1, 1))
                cols_ref[c, start : start + rows, :] = swapped.astype(bf16)


def edges(state, shear, perm):
    _, height, count, width = state.shape
    whole = lambda *shape: pl.BlockSpec(shape, lambda i: (0,) * len(shape))
    return pl.pallas_call(
        edges_kernel,
        grid=(height // EDGE,),
        in_specs=[
            pl.BlockSpec((4, EDGE, count, width), lambda i: (0, i, 0, 0)),
            pl.BlockSpec((EDGE, count, width), lambda i: (i, 0, 0)),
            pl.BlockSpec((EDGE, count, width), lambda i: (i, 0, 0)),
        ],
        out_specs=[whole(6, count, width), *[whole(6, height, width)] * 4],
        out_shape=[
            jax.ShapeDtypeStruct((6, count, width), bf16),
            *[jax.ShapeDtypeStruct((6, height, width), f32)] * 4,
        ],
        scratch_shapes=[pltpu.VMEM((6, count, width), f32), pltpu.VMEM((EDGE * width, width), bf16)],
        compiler_params=params(),
        name="edges",
    )(state, shear, perm)


def neighbours(cols, first, low, high, last):
    n_rad = lax.axis_size("rad")
    n_az = lax.axis_size("az")
    from_right = lax.ppermute(cols, "rad", [(i + 1, i) for i in range(n_rad - 1)])
    from_left = lax.ppermute(cols, "rad", [(i, i + 1) for i in range(n_rad - 1)])
    before = lax.ppermute(last, "az", [(i, (i + 1) % n_az) for i in range(n_az)])
    after = lax.ppermute(first, "az", [((i + 1) % n_az, i) for i in range(n_az)])
    beside = jnp.where(lanes_of(cols.shape) % 2 == 0, from_right, from_left)
    return beside, before, after, low, high


def stage(scratch, center, above, below, before, after, step, steps, slab, count):
    top = jnp.where(step > 0, 1.0, 0.0)
    bottom = jnp.where(step < steps - 1, 1.0, 0.0)
    scratch[0, 8 : 8 + count, :] = above[...].astype(f32) * top
    scratch[slab + 1, 8 : 8 + count, :] = below[...].astype(f32) * bottom
    for i in range(slab):
        scratch[i + 1, 8 : 8 + count, :] = center[i].astype(f32)
        if before is not None:
            h = step * slab + i
            scratch[i + 1, 7:8, :] = before[pl.ds(h, 1), :]
            scratch[i + 1, 8 + count : 9 + count, :] = after[pl.ds(h, 1), :]


def radial_pair(x, beside, shift, lane):
    width = x.shape[1]
    beside = pltpu.roll(beside, shift, 1)
    right = jnp.where(lane == width - 1, beside, pltpu.roll(x, width - 1, 1))
    left = jnp.where(lane == 0, beside, pltpu.roll(x, 1, 1))
    return right.astype(f32), left.astype(f32)


def weighted(center, faces, around):
    total = faces[1][0] * around[0]
    for face, other in zip(faces[1][1:], around[1:]):
        total = total + face * other
    return faces[0] * center - total


def total_of(values):
    total = values[0]
    for value in values[1:]:
        total = total + value
    return total


def fluid_kernel(
    shared, p_ref, p_up, p_dn, k_ref, k_up, k_dn, z_ref, z_up, z_dn, r_ref, t_ref, src_ref,
    beside_ref, before_ref, after_ref, cos_ref,
    *rest,
):
    outs, (sum_ref, ps, ks, zs, ts, res) = rest[shared:-6], rest[-6:]
    step = pl.program_id(0)
    slab, count, width = src_ref.shape
    height = before_ref.shape[1]
    steps = height // slab
    tile, levels, _ = outs[0].shape

    @pl.when(step == 0)
    def _():
        sum_ref[...] = jnp.zeros_like(sum_ref)

    @pl.when(step < steps)
    def _():
        stage(ps, p_ref.at[0], p_up.at[0, 0], p_dn.at[0, 0], before_ref.at[3], after_ref.at[3], step, steps, slab, count)
        stage(ks, k_ref, k_up.at[0], k_dn.at[0], before_ref.at[5], after_ref.at[5], step, steps, slab, count)
        stage(zs, z_ref.at[0], z_up.at[0, 0], z_dn.at[0, 0], None, None, step, steps, slab, count)
        for i in range(slab):
            h = step * slab + i
            ts[i, 8 : 8 + count, :] = t_ref[0, i].astype(f32)
            ts[i, 7:8, :] = before_ref[1, pl.ds(h, 1), :]
            ts[i, 8 + count : 9 + count, :] = after_ref[1, pl.ds(h, 1), :]
        lane = lanes_of((ROWS, width))

        def plane(i, total):
            h = step * slab + i
            shift = 2 * height - 1 - 2 * h
            for a in range(0, count, ROWS):
                at = slice(8 + a, 8 + a + ROWS)
                prev = slice(7 + a, 7 + a + ROWS)
                nxt = slice(9 + a, 9 + a + ROWS)
                own = slice(a, a + ROWS)
                p = ps[i + 1, at, :]
                k = ks[i + 1, at, :]
                p_r, p_l = radial_pair(p_ref[0, i, own, :], beside_ref[3, own, :], shift, lane)
                k_r, k_l = radial_pair(k_ref[i, own, :], beside_ref[5, own, :], shift, lane)
                others = [ks[i + 1, nxt, :], ks[i + 1, prev, :], ks[i + 2, at, :], ks[i, at, :]]
                faces = [k + other for other in (k_r, k_l, *others)]
                around = [ps[i + 1, nxt, :], ps[i + 1, prev, :], ps[i + 2, at, :], ps[i, at, :]]
                flux = weighted(p, (total_of(faces), faces), (p_r, p_l, *around))
                u_r, u_l = radial_pair(r_ref[0, i, own, :], beside_ref[0, own, :], shift, lane)
                spread = (u_r - u_l) + (ts[i, nxt, :] - ts[i, prev, :])
                spread += zs[i + 2, at, :] - zs[i, at, :]
                if biot_coupling != 2.0:
                    spread = (0.5 * biot_coupling) * spread
                value = (src_ref[i, own, :].astype(f32) + spread) + (storage * p + 0.5 * flux)
                res[h, own, :] = value
                total = total + fold(value * value)
            return total

        sum_ref[...] += lax.fori_loop(0, slab, plane, jnp.zeros((8, width), f32), unroll=4)

    @pl.when(step >= steps)
    def _():
        base = (step - steps) * tile

        def group(j, carry):
            start = pl.multiple_of(base + 8 * j, 8)
            columns = [
                jnp.swapaxes(res[h : h + 8, pl.ds(start, 8), :], 0, 1) for h in range(0, height, 8)
            ]
            for pair in range(4):
                highs, lows = [], []
                for s in range(2):
                    x = jnp.concatenate([column[2 * pair + s] for column in columns], axis=0)
                    high, low = split(x)
                    highs.append(high)
                    lows.append(low)
                high = jnp.concatenate(highs, axis=1)
                low = jnp.concatenate(lows, axis=1)
                stacked = jnp.concatenate([high, low, high], axis=0)
                y = jnp.dot(cos_ref[...], stacked, preferred_element_type=f32)
                for s in range(2):
                    for block, out in enumerate(outs):
                        out[8 * j + 2 * pair + s, :, :] = y[
                            block * levels : (block + 1) * levels, s * width : (s + 1) * width
                        ]
            return carry

        lax.fori_loop(0, tile // 8, group, 0)


def plane_specs(channel, slab, steps, count, width, base=0, part=0):
    at = lambda i: jnp.minimum(i + base, steps - 1)
    up = lambda i: jnp.maximum(at(i) * slab - 1, 0)
    down = lambda i: jnp.minimum(at(i) * slab + slab, steps * slab - 1)
    if channel is None:
        return [
            pl.BlockSpec((slab, count, width), lambda i: (at(i), part, 0)),
            pl.BlockSpec((1, count, width), lambda i: (up(i), part, 0)),
            pl.BlockSpec((1, count, width), lambda i: (down(i), part, 0)),
        ]
    return [
        pl.BlockSpec((1, slab, count, width), lambda i: (channel, at(i), part, 0)),
        pl.BlockSpec((1, 1, count, width), lambda i: (channel, up(i), part, 0)),
        pl.BlockSpec((1, 1, count, width), lambda i: (channel, down(i), part, 0)),
    ]


def fluid(state, source, perm, beside, before, after, table, parts, half, shared):
    _, height, whole_count, width = state.shape
    count = whole_count // HALVES
    steps = height // FLUID
    tile = min(TILE, count)
    pieces = parts * CHUNKS
    levels = height // pieces
    specs = lambda c: plane_specs(c, FLUID, steps, count, width, part=half)
    whole = lambda x: pl.BlockSpec(x.shape, lambda i: (0,) * x.ndim)
    at = lambda first: pl.BlockSpec(
        (tile, levels, width), lambda i: (first + jnp.maximum(i - steps, 0), 0, 0)
    )
    rest = pieces - parts
    return pl.pallas_call(
        functools.partial(fluid_kernel, len(shared)),
        grid=(steps + count // tile,),
        in_specs=[
            *specs(3), *specs(None), *specs(2), specs(0)[0], specs(1)[0], specs(None)[0],
            pl.BlockSpec((6, count, width), lambda i: (0, half, 0)), whole(before), whole(after), whole(table),
            *[pl.BlockSpec(memory_space=pl.ANY)] * len(shared),
        ],
        out_specs=[
            *[at(0)] * parts, *[at(half * (count // tile))] * rest,
            pl.BlockSpec((8, width), lambda i: (0, 0)),
        ],
        out_shape=[
            *[jax.ShapeDtypeStruct((count, levels, width), f32)] * parts,
            *[jax.ShapeDtypeStruct((whole_count, levels, width), f32)] * rest,
            jax.ShapeDtypeStruct((8, width), f32),
        ],
        scratch_shapes=[
            pltpu.VMEM((FLUID + 2, count + 16, width), f32),
            pltpu.VMEM((FLUID + 2, count + 16, width), f32),
            pltpu.VMEM((FLUID + 2, count + 16, width), f32),
            pltpu.VMEM((FLUID, count + 16, width), f32),
            pltpu.VMEM((height, count, width), f32),
        ],
        input_output_aliases={16 + i: pieces - len(shared) + i for i in range(len(shared))},
        compiler_params=params(),
        name="fluid",
    )(state, state, state, perm, perm, perm, state, state, state, state, state, source,
      beside, before, after, table, *shared)


def momentum_kernel(base, steps, priors, *refs):
    fields = [refs[3 * c : 3 * c + 3] for c in range(5)]
    beside_ref, before_ref, after_ref = refs[15:18]
    prior_refs = refs[18 : 18 + priors]
    *_, out_ref, rr_ref, rz_ref = refs[:-5]
    scratch = refs[-5:]
    step = pl.program_id(0) + base
    _, slab, count, width = out_ref.shape
    height = before_ref.shape[1]

    @pl.when(step == base)
    def _():
        rr_ref[...] = total_of([prior[...] for prior in prior_refs[::2]])
        rz_ref[...] = total_of([prior[...] for prior in prior_refs[1::2]])

    for c in range(5):
        center, up, down = fields[c]
        if c < 4:
            center, up, down = center.at[0], up.at[0, 0], down.at[0, 0]
        else:
            up, down = up.at[0], down.at[0]
        stage(scratch[c], center, up, down, before_ref.at[c], after_ref.at[c], step, steps, slab, count)
    lane = lanes_of((ROWS, width))

    def plane(i, totals):
        rr, rz = totals
        h = step * slab + i
        shift = 2 * height - 1 - 2 * h
        for a in range(0, count, ROWS):
            at = slice(8 + a, 8 + a + ROWS)
            prev = slice(7 + a, 7 + a + ROWS)
            nxt = slice(9 + a, 9 + a + ROWS)
            own = slice(a, a + ROWS)

            def around(c):
                s = scratch[c]
                center = fields[c][0].at[0] if c < 4 else fields[c][0]
                right, left = radial_pair(center[i, own, :], beside_ref[c, own, :], shift, lane)
                others = [s[i + 1, nxt, :], s[i + 1, prev, :], s[i + 2, at, :], s[i, at, :]]
                return s[i + 1, at, :], (right, left, *others)

            g, g_around = around(4)
            faces = [g + other for other in g_around]
            diagonal = total_of(faces)
            inverse = -1.0 / diagonal
            _, p = around(3)
            squares = None
            for c in range(3):
                u, u_around = around(c)
                value = weighted(u, (diagonal, faces), u_around)
                value = value + biot_coupling * (p[2 * c] - p[2 * c + 1])
                out_ref[c, i, own, :] = value * inverse
                squares = value * value if squares is None else squares + value * value
            rr = rr + fold(squares)
            rz = rz + fold(squares * inverse)
        return rr, rz

    zero = jnp.zeros((8, width), f32)
    rr, rz = lax.fori_loop(0, slab, plane, (zero, zero), unroll=2)
    rr_ref[...] += 0.25 * rr
    rz_ref[...] -= 0.5 * rz


def momentum(state, shear, beside, before, after, piece, prior, rows=None):
    _, height, count, width = state.shape
    steps = height // SLAB
    base, end = ((eighth * steps) // 8 for eighth in piece)
    specs = lambda c: plane_specs(c, SLAB, steps, count, width, base=base)
    whole = lambda x: pl.BlockSpec(x.shape, lambda i: (0,) * x.ndim)
    operands = [*[state] * 12, shear, shear, shear, beside, before, after, *prior]
    in_specs = [
        *specs(0), *specs(1), *specs(2), *specs(3), *specs(None),
        *[whole(x) for x in operands[15:]],
    ]
    aliases = {}
    if rows is not None:
        aliases = {len(operands): 0}
        operands.append(rows)
        in_specs.append(pl.BlockSpec(memory_space=pl.ANY))
    return pl.pallas_call(
        functools.partial(momentum_kernel, base, steps, len(prior)),
        grid=(end - base,),
        in_specs=in_specs,
        out_specs=[
            pl.BlockSpec((3, SLAB, count, width), lambda i: (0, i + base, 0, 0)),
            pl.BlockSpec((8, width), lambda i: (0, 0)),
            pl.BlockSpec((8, width), lambda i: (0, 0)),
        ],
        out_shape=[
            jax.ShapeDtypeStruct((3, height, count, width), f32),
            jax.ShapeDtypeStruct((8, width), f32),
            jax.ShapeDtypeStruct((8, width), f32),
        ],
        scratch_shapes=[pltpu.VMEM((SLAB + 2, count + 16, width), f32)] * 5,
        input_output_aliases=aliases,
        compiler_params=params(),
        name="momentum",
    )(*operands)


def product(x, high_ref, low_ref):
    high, low = split(x)
    y = jnp.dot(high, high_ref[...], preferred_element_type=f32)
    y = y + jnp.dot(low, high_ref[...], preferred_element_type=f32)
    return y + jnp.dot(high, low_ref[...], preferred_element_type=f32)


def modes_kernel(groups, *refs):
    slabs, (high_ref, low_ref, ratio_ref, x_ref, all_ref, ends_ref, power) = refs[:-7], refs[-7:]
    step = pl.program_id(0)
    tile, levels, width = slabs[0].shape

    @pl.when(step == 0)
    def _():
        ends_ref[...] = jnp.zeros_like(ends_ref)
        power[...] = jnp.ones_like(power)

    each = len(slabs) // groups
    span = pl.num_programs(0) // groups
    for half in range(groups):

        @pl.when((step >= half * span) & (step < (half + 1) * span))
        def _():
            mine = slabs[half * each : (half + 1) * each]
            lines = jnp.concatenate([slab[...].reshape(tile * levels, width) for slab in mine], axis=1)
            x_ref[...] = product(lines, high_ref, low_ref).reshape(x_ref.shape)

    ratio = ratio_ref[...]

    def scan(a, carry):
        forward, backward, weight = carry
        x = x_ref[a]
        return x + ratio * forward, backward + weight * x, weight * ratio

    forward, backward, weight = lax.fori_loop(
        0, tile, scan, (ends_ref[0], ends_ref[1], power[...]), unroll=4
    )
    ends_ref[0] = forward
    ends_ref[1] = backward
    power[...] = weight

    @pl.when(step == pl.num_programs(0) - 1)
    def _():
        for shard in range(all_ref.shape[0]):
            all_ref[shard] = ends_ref[...]


def modes(groups, high, low, ratio, shards):
    slabs = sum(groups, [])
    span, levels, width = slabs[0].shape
    count = span * len(groups)
    tile = min(TILE, span)
    total = high.shape[1]
    steps = span // tile
    at = lambda half: pl.BlockSpec(
        (tile, levels, width), lambda i: (jnp.clip(i - half * steps, 0, steps - 1), 0, 0)
    )
    whole = lambda x: pl.BlockSpec(x.shape, lambda i: (0,) * x.ndim)
    return pl.pallas_call(
        functools.partial(modes_kernel, len(groups)),
        grid=(count // tile,),
        in_specs=[
            *[at(half) for half, group in enumerate(groups) for _ in group],
            whole(high), whole(low), whole(ratio),
        ],
        out_specs=[
            pl.BlockSpec((tile, levels, total), lambda i: (i, 0, 0)),
            pl.BlockSpec((shards, 2, levels, total), lambda i: (0, 0, 0, 0)),
        ],
        out_shape=[
            jax.ShapeDtypeStruct((count, levels, total), f32),
            jax.ShapeDtypeStruct((shards, 2, levels, total), f32),
        ],
        scratch_shapes=[pltpu.VMEM((2, levels, total), f32), pltpu.VMEM((levels, total), f32)],
        compiler_params=params(),
        name="modes",
    )(*slabs, high, low, ratio)


def solve_kernel(
    last, place_ref, x_ref, ends_ref, ratio_ref, gain_ref, span_ref, high_ref, low_ref,
    rr_ref, rz_ref, prior_ref, *rest,
):
    outs, (all_ref, sum_ref, lines, tail, carry_ref, block) = rest[:-6], rest[-6:]
    step = pl.program_id(0)
    half = pl.num_programs(0) // 2
    shards = ends_ref.shape[0]
    tile, levels, total = x_ref.shape
    width = outs[0].shape[2]
    ratio = ratio_ref[...]

    @pl.when(step == 0)
    def _():
        span = span_ref[...]
        place = place_ref[0]
        weight = jnp.ones_like(span)
        forward = jnp.zeros_like(span)
        backward = jnp.zeros_like(span)
        for j in range(1, shards + 1):
            forward += weight * ends_ref[lax.rem(place - j + shards, shards), 0]
            backward += weight * ends_ref[lax.rem(place + j, shards), 1]
            weight = weight * span
        carry_ref[...] = forward / (1.0 - weight)
        tail[...] = backward / (1.0 - weight)
        sum_ref[...] = jnp.zeros_like(sum_ref)

    @pl.when(step < half)
    def _():
        def scan(a, y):
            y = x_ref[a] + ratio * y
            lines[step * tile + a] = y
            return y

        carry_ref[...] = lax.fori_loop(0, tile, scan, carry_ref[...], unroll=4)

    @pl.when(step == half)
    def _():
        carry_ref[...] = gain_ref[...] * (ratio * carry_ref[...] + tail[...])

    @pl.when(step >= half)
    def _():
        base = (2 * half - 1 - step) * tile

        def scan(j, carry):
            q, dot = carry
            a = tile - 1 - j
            q = ratio * (lines[base + a] + q)
            block[a] = q
            return q, dot + x_ref[a] * q

        zero = jnp.zeros((levels, total), f32)
        q, dot = lax.fori_loop(0, tile, scan, (carry_ref[...], zero), unroll=4)
        carry_ref[...] = q
        sum_ref[...] += dot
        back = product(block[...].reshape(tile * levels, total), high_ref, low_ref)
        span = half // (len(outs) * width // total)
        for index, out in enumerate(outs):
            group, part = divmod(index, total // width)

            @pl.when((base >= group * span * tile) & (base < (group + 1) * span * tile))
            def _():
                out[...] = back[:, part * width : (part + 1) * width].reshape(tile, levels, width)

    @pl.when(step == 2 * half - 1)
    def _():
        dots = fold(sum_ref[...])
        lanes = dots[:, :width]
        for start in range(width, total, width):
            lanes = lanes + dots[:, start : start + width]
        sums = lanes + prior_ref[...]
        if last:
            row = lax.broadcasted_iota(jnp.int32, (8, width), 0)
            rr = jnp.sum(rr_ref[...], axis=0, keepdims=True)
            rz = jnp.sum(rz_ref[...] + sums, axis=0, keepdims=True)
            sums = jnp.where(row == 0, rr, jnp.where(row == 1, rz, 0.0))
        for device in range(all_ref.shape[0]):
            all_ref[device] = sums


def solve(place, x, ends, ratio, gain, span, high, low, rr, rz, prior, parts, copies, last):
    groups = HALVES if last else 1
    count, levels, total = x.shape
    tile = min(TILE, count // groups)
    half = count // tile
    width = total // parts
    whole = lambda v: pl.BlockSpec(v.shape, lambda i, s: (0,) * v.ndim)
    back = lambda i: jnp.minimum(2 * half - 1 - i, half - 1)
    share = half // groups
    out_at = lambda group: pl.BlockSpec(
        (tile, levels, width), lambda i, s: (jnp.clip(back(i) - group * share, 0, share - 1), 0, 0)
    )
    return pl.pallas_call(
        functools.partial(solve_kernel, last),
        grid_spec=pltpu.PrefetchScalarGridSpec(
            num_scalar_prefetch=1,
            grid=(2 * half,),
            in_specs=[
                pl.BlockSpec((tile, levels, total), lambda i, s: (jnp.minimum(i, 2 * half - 1 - i), 0, 0)),
                whole(ends), whole(ratio), whole(gain), whole(span), whole(high), whole(low), whole(rr), whole(rz), whole(prior),
            ],
            out_specs=[
                *[out_at(group) for group in range(groups) for _ in range(parts)],
                pl.BlockSpec((copies, 8, width), lambda i, s: (0, 0, 0)),
            ],
            scratch_shapes=[
                pltpu.VMEM((levels, total), f32),
                pltpu.VMEM((count, levels, total), f32),
                pltpu.VMEM((levels, total), f32),
                pltpu.VMEM((levels, total), f32),
                pltpu.VMEM((tile, levels, total), f32),
            ],
        ),
        out_shape=[
            *[jax.ShapeDtypeStruct((count // groups, levels, width), f32)] * (parts * groups),
            jax.ShapeDtypeStruct((copies, 8, width), f32),
        ],
        compiler_params=params(),
        name="solve",
    )(place, x, ends, ratio, gain, span, high, low, rr, rz, prior)


def scale_kernel(alpha_ref, in_ref, out_ref):
    out_ref[...] = (alpha_ref[0] * in_ref[...]).astype(bf16)


def scale_rows(alpha, moment):
    _, height, count, width = moment.shape
    return pl.pallas_call(
        scale_kernel,
        grid_spec=pltpu.PrefetchScalarGridSpec(
            num_scalar_prefetch=1,
            grid=(3 * height // 16,),
            in_specs=[pl.BlockSpec((1, 16, count, width), lambda i, s: (i // (height // 16), i % (height // 16), 0, 0))],
            out_specs=pl.BlockSpec((1, 16, count, width), lambda i, s: (i // (height // 16), i % (height // 16), 0, 0)),
        ),
        out_shape=jax.ShapeDtypeStruct((4, height, count, width), bf16),
        compiler_params=params(),
        name="scale_rows",
    )(alpha, moment)


def pressure_kernel(alpha_ref, *refs):
    pieces, (cos_ref, rest_ref, out_ref) = refs[:-3], refs[-3:]
    tile, levels, width = pieces[0].shape
    height = levels * len(pieces)
    alpha = alpha_ref[0]

    def group(j, carry):
        planes = []
        for pair in range(8):
            highs, lows = [], []
            for s in range(2):
                a = 16 * j + 2 * pair + s
                x = jnp.concatenate([piece[a] for piece in pieces], axis=0)
                high, low = split(x)
                highs.append(high)
                lows.append(low)
            high = jnp.concatenate(highs, axis=1)
            low = jnp.concatenate(lows, axis=1)
            stacked = jnp.concatenate([high, low, high], axis=0)
            y = alpha * jnp.dot(cos_ref[...], stacked, preferred_element_type=f32)
            planes += [y[:, :width], y[:, width:]]
        start = pl.multiple_of(16 * j, 16)
        for h in range(0, height, 8):
            low = jnp.swapaxes(jnp.stack([y[h : h + 8] for y in planes[:8]]), 0, 1)
            high = jnp.swapaxes(jnp.stack([y[h : h + 8] for y in planes[8:]]), 0, 1)
            block = jnp.concatenate([low, high], axis=1)
            out_ref[0, h : h + 8, pl.ds(start, 16), :] = block.astype(bf16)
        return carry

    lax.fori_loop(0, tile // 16, group, 0)


def pressure_rows(alpha, planes, table, out, half):
    _, height, whole_count, width = out.shape
    count = whole_count // HALVES
    tile = min(TILE, count)
    first = half * (count // tile)
    at = lambda x: pl.BlockSpec(
        (tile, *x.shape[1:]), lambda i, s: (i if x.shape[0] == count else first + i, 0, 0)
    )
    return pl.pallas_call(
        pressure_kernel,
        grid_spec=pltpu.PrefetchScalarGridSpec(
            num_scalar_prefetch=1,
            grid=(count // tile,),
            in_specs=[
                *[at(x) for x in planes],
                pl.BlockSpec(table.shape, lambda i, s: (0, 0)),
                pl.BlockSpec(memory_space=pl.ANY),
            ],
            out_specs=pl.BlockSpec((1, height, tile, width), lambda i, s: (3, 0, first + i, 0)),
        ),
        out_shape=jax.ShapeDtypeStruct(out.shape, bf16),
        input_output_aliases={len(planes) + 2: 0},
        compiler_params=params(),
        name="pressure_rows",
    )(alpha, *planes, table, out)


def cosine_table(extent):
    row_ids = jnp.arange(extent, dtype=f32)[:, None]
    col_ids = jnp.arange(extent, dtype=f32)[None, :]
    scaled = jnp.where(row_ids == 0, math.sqrt(1.0 / extent), math.sqrt(2.0 / extent))
    return scaled * jnp.cos(math.pi * (col_ids + 0.5) * row_ids / extent)


def pairwise(pieces, axis):
    count = lax.axis_size(axis)
    return [pieces[0]] + [
        lax.ppermute(pieces[s], axis, [(i, i ^ s) for i in range(count)]) for s in range(1, count)
    ]


def exchanged(copies, axis):
    return lax.all_to_all(copies, axis, split_axis=0, concat_axis=0, tiled=True)


def fence(*values):
    return lax.optimization_barrier(values)


def step(state, source, shear, permeability, radial_basis, radial_eigen):
    _, height, count, width = state.shape
    parts = lax.axis_size("rad")
    levels = height // parts // CHUNKS
    owner = lax.axis_index("rad") ^ jnp.arange(parts, dtype=jnp.int32)
    cosine = cosine_table(height).reshape(parts, CHUNKS, levels, height)
    cosine = jnp.swapaxes(jnp.take(cosine, owner, axis=0), 0, 1).reshape(height, height)
    high, low = split_table(cosine)
    table = jnp.concatenate([high, high, low], axis=1)

    cols, first, *others = edges(state, shear, permeability)
    first, radial_basis = fence(first, radial_basis)
    beside, before, after, mid_low, mid_high = neighbours(cols, first, *others)
    blocks = pairwise([radial_basis] * parts, "rad")
    sent, priors, shared = [], [], []
    for half, ends in enumerate(((before, mid_high), (mid_low, after))):
        *heights, fluid_rr = fluid(
            state, source, permeability, beside, *ends, table, parts, half, shared
        )
        shared = heights[parts:]
        sent.append(pairwise(heights[:parts], "rad"))
        priors += [fluid_rr, jnp.zeros_like(fluid_rr)]
    slabs = [sent]
    for chunk in range(1, CHUNKS):
        slabs.append([pairwise(shared[(chunk - 1) * parts : chunk * parts], "rad")])
    high, low = split_table(jnp.concatenate(blocks))
    around = (beside, before, after)
    moment, rr, rz = momentum(state, shear, *around, (0, 2), priors)

    place = lax.axis_index("az").reshape(1)
    shards = lax.axis_size("az")
    sums = jnp.zeros((8, width), f32)
    planes = []
    for chunk in range(CHUNKS):
        first = (lax.axis_index("rad") * CHUNKS + chunk) * levels
        level = (first + jnp.arange(levels, dtype=jnp.int32)).astype(f32)
        height_eigen = 4.0 * jnp.sin(math.pi * level / (2.0 * height)) ** 2
        center = storage + radial_eigen[None, :] + height_eigen[:, None]
        root = jnp.sqrt(center * (center + 4.0))
        ratio = 2.0 / (center + 2.0 + root)
        span = lax.integer_pow(ratio, count)
        x, ends = modes(slabs[chunk], high, low, ratio, shards)
        ends = exchanged(ends, "az")
        piece = ((2, 3), (6, 8))[chunk]
        moment, rr, rz = momentum(state, shear, *around, piece, (rr, rz), moment)
        last = chunk == CHUNKS - 1
        copies = shards * parts if last else 1
        *back, sums = solve(
            place, x, ends, ratio, 1.0 / root, span, high.T, low.T, rr, rz, sums, parts, copies, last
        )
        if last:
            sums = exchanged(sums, ("az", "rad"))
        else:
            sums = sums[0]
            moment, rr, rz = momentum(state, shear, *around, (3, 6), (rr, rz), moment)
        if last:
            backs = [None] * HALVES
            for half in reversed(range(HALVES)):
                backs[half] = pairwise(back[half * parts : (half + 1) * parts], "rad")
        else:
            planes += pairwise(back, "rad")
    totals = jnp.sum(sums, axis=(0, 2))
    alpha = (totals[0] / totals[1]).reshape(1)
    out = scale_rows(alpha, moment)
    high, low = split_table(cosine.T)
    table = jnp.concatenate([high, high, low], axis=1)
    for half in reversed(range(HALVES)):
        out = pressure_rows(alpha, planes + backs[half], table, out, half)
    return out


def solution(mesh):
    placed = (
        P(None, None, "az", "rad"),
        P(None, "az", "rad"),
        P(None, "az", "rad"),
        P(None, "az", "rad"),
        P("rad", None),
        P(),
    )
    return jax.shard_map(
        step, mesh=mesh, in_specs=placed, out_specs=P(None, None, "az", "rad"), check_vma=False
    )
```

```python
import functools
import math

import jax
import jax.numpy as jnp
from jax import lax
from jax.experimental import pallas as pl
from jax.experimental.pallas import tpu as pltpu
from jax.sharding import PartitionSpec as P


biot_coupling = 2.0
storage = 1.0

f32 = jnp.float32
bf16 = jnp.bfloat16


SLAB = 8
FLUID = 16
PICKED = (1, 2, 4)
EDGE = 16
ROWS = 16
TILE = 64
TAIL = 4
HALVES = 2
CHUNKS = 2


def params(limit=56):
    return pltpu.CompilerParams(
        dimension_semantics=("arbitrary",), vmem_limit_bytes=limit * 1024 * 1024
    )


def lanes_of(shape):
    return lax.broadcasted_iota(jnp.int32, shape, len(shape) - 1)


def split(x):
    high = x.astype(bf16)
    low = (x - high.astype(f32)).astype(bf16)
    return high, low


def fold(x):
    total = x[0:8]
    for start in range(8, x.shape[0], 8):
        total = total + x[start : start + 8]
    return total


def split_table(x):
    rounded = lax.reduce_precision(x, exponent_bits=8, mantissa_bits=7)
    return rounded.astype(bf16), (x - rounded).astype(bf16)


def edges_kernel(state_ref, shear_ref, perm_ref, cols_ref, *rest):
    *row_outs, acc, chosen = rest[:-4]
    row_refs = rest[-4:]
    step = pl.program_id(0)
    slab, count, width = shear_ref.shape
    rows = min(64, count // 2)
    places = (0, count // 2 - 1, count // 2, count - 1)
    lane = lanes_of((rows, width))
    sources = [state_ref.at[c] if c < 4 else (shear_ref, perm_ref)[c - 4] for c in range(6)]

    @pl.when(step == 0)
    def _():
        row = lax.broadcasted_iota(jnp.int32, (slab * width, width), 0)
        plane = lax.div(row, width)
        spot = lax.rem(row, width)
        column = lanes_of((slab * width, width))
        wanted = (spot == 0) & (column == 2 * plane + 1) | (spot == width - 1) & (column == 2 * plane)
        chosen[...] = jnp.where(wanted, 1.0, 0.0).astype(bf16)
        for c in PICKED:
            acc[c] = jnp.zeros_like(acc[c])

    for c in PICKED:
        src = sources[c]
        planes = jnp.concatenate([src[i] for i in range(slab)], axis=1)
        packed = jnp.dot(planes, chosen[...], preferred_element_type=f32)
        acc[c] += pltpu.roll(packed, 2 * slab * step, 1)
        for i in range(slab):
            h = step * slab + i
            for place, row_ref in zip(places, row_refs):
                start = place // 16 * 16
                x = src[i, start : start + 16, :].astype(f32)
                row_ref[c, pl.ds(h, 1), :] = x[place - start : place - start + 1]

    for c in range(6):
        if c in PICKED:
            continue
        src = sources[c]
        for start in range(0, count, rows):
            value = acc[c, start : start + rows, :]
            for i in range(slab):
                h = step * slab + i
                x = src[i, start : start + rows, :].astype(f32)
                value = jnp.where((lane >> 1) == h, pltpu.roll(x, 2 * h + 1, 1), value)
                for place, row_ref in zip(places, row_refs):
                    if start <= place < start + rows:
                        row_ref[c, pl.ds(h, 1), :] = x[place - start : place - start + 1]
            acc[c, start : start + rows, :] = value

    @pl.when(step == pl.num_programs(0) - 1)
    def _():
        for out, row_ref in zip(row_outs, row_refs):
            out[...] = row_ref[...].astype(bf16)
        for c in range(6):
            for start in range(0, count, rows):
                v = acc[c, start : start + rows, :]
                swapped = jnp.where(lane % 2 == 0, pltpu.roll(v, width - 1, 1), pltpu.roll(v, 1, 1))
                cols_ref[c, start : start + rows, :] = swapped.astype(bf16)


def edges(state, shear, perm):
    _, height, count, width = state.shape
    whole = lambda *shape: pl.BlockSpec(shape, lambda i: (0,) * len(shape))
    return pl.pallas_call(
        edges_kernel,
        grid=(height // EDGE,),
        in_specs=[
            pl.BlockSpec((4, EDGE, count, width), lambda i: (0, i, 0, 0)),
            pl.BlockSpec((EDGE, count, width), lambda i: (i, 0, 0)),
            pl.BlockSpec((EDGE, count, width), lambda i: (i, 0, 0)),
        ],
        out_specs=[whole(6, count, width), *[whole(6, height, width)] * 4],
        out_shape=[
            jax.ShapeDtypeStruct((6, count, width), bf16),
            *[jax.ShapeDtypeStruct((6, height, width), bf16)] * 4,
        ],
        scratch_shapes=[
            pltpu.VMEM((6, count, width), f32),
            pltpu.VMEM((EDGE * width, width), bf16),
            *[pltpu.VMEM((6, height, width), f32)] * 4,
        ],
        compiler_params=params(),
        name="edges",
    )(state, shear, perm)


def neighbours(cols, first, low, high, last):
    n_rad = lax.axis_size("rad")
    n_az = lax.axis_size("az")
    from_right = lax.ppermute(cols, "rad", [(i + 1, i) for i in range(n_rad - 1)])
    from_left = lax.ppermute(cols, "rad", [(i, i + 1) for i in range(n_rad - 1)])
    before = lax.ppermute(last, "az", [(i, (i + 1) % n_az) for i in range(n_az)])
    after = lax.ppermute(first, "az", [((i + 1) % n_az, i) for i in range(n_az)])
    beside = jnp.where(lanes_of(cols.shape) % 2 == 0, from_right, from_left)
    return beside, before, after, low, high


def stage(scratch, center, above, below, before, after, step, steps, slab, count):
    top = jnp.where(step > 0, 1.0, 0.0)
    bottom = jnp.where(step < steps - 1, 1.0, 0.0)
    scratch[0, 8 : 8 + count, :] = above[...].astype(f32) * top
    scratch[slab + 1, 8 : 8 + count, :] = below[...].astype(f32) * bottom
    for i in range(slab):
        scratch[i + 1, 8 : 8 + count, :] = center[i].astype(f32)
        if before is not None:
            h = step * slab + i
            scratch[i + 1, 7:8, :] = before[pl.ds(h, 1), :]
            scratch[i + 1, 8 + count : 9 + count, :] = after[pl.ds(h, 1), :]


def radial_pair(x, beside, shift, lane):
    width = x.shape[1]
    beside = pltpu.roll(beside, shift, 1)
    right = jnp.where(lane == width - 1, beside, pltpu.roll(x, width - 1, 1))
    left = jnp.where(lane == 0, beside, pltpu.roll(x, 1, 1))
    return right.astype(f32), left.astype(f32)


def weighted(center, faces, around):
    total = faces[1][0] * around[0]
    for face, other in zip(faces[1][1:], around[1:]):
        total = total + face * other
    return faces[0] * center - total


def total_of(values):
    total = values[0]
    for value in values[1:]:
        total = total + value
    return total


def fluid_kernel(
    shared, p_ref, p_up, p_dn, k_ref, k_up, k_dn, z_ref, z_up, z_dn, r_ref, t_ref, src_ref,
    beside_ref, before_in, after_in, cos_ref,
    *rest,
):
    outs = rest[shared:-8]
    sum_ref, ps, ks, zs, ts, res, before_ref, after_ref = rest[-8:]
    step = pl.program_id(0)
    slab, count, width = src_ref.shape
    height = before_ref.shape[1]
    steps = height // slab
    tile, levels, _ = outs[0].shape

    @pl.when(step == 0)
    def _():
        sum_ref[...] = jnp.zeros_like(sum_ref)
        before_ref[...] = before_in[...].astype(f32)
        after_ref[...] = after_in[...].astype(f32)

    @pl.when(step < steps)
    def _():
        stage(ps, p_ref.at[0], p_up.at[0, 0], p_dn.at[0, 0], before_ref.at[3], after_ref.at[3], step, steps, slab, count)
        stage(ks, k_ref, k_up.at[0], k_dn.at[0], before_ref.at[5], after_ref.at[5], step, steps, slab, count)
        stage(zs, z_ref.at[0], z_up.at[0, 0], z_dn.at[0, 0], None, None, step, steps, slab, count)
        for i in range(slab):
            h = step * slab + i
            ts[i, 8 : 8 + count, :] = t_ref[0, i].astype(f32)
            ts[i, 7:8, :] = before_ref[1, pl.ds(h, 1), :]
            ts[i, 8 + count : 9 + count, :] = after_ref[1, pl.ds(h, 1), :]
        lane = lanes_of((ROWS, width))

        def plane(i, total):
            h = step * slab + i
            shift = 2 * height - 1 - 2 * h
            for a in range(0, count, ROWS):
                at = slice(8 + a, 8 + a + ROWS)
                prev = slice(7 + a, 7 + a + ROWS)
                nxt = slice(9 + a, 9 + a + ROWS)
                own = slice(a, a + ROWS)
                p = ps[i + 1, at, :]
                k = ks[i + 1, at, :]
                p_r, p_l = radial_pair(p_ref[0, i, own, :], beside_ref[3, own, :], shift, lane)
                k_r, k_l = radial_pair(k_ref[i, own, :], beside_ref[5, own, :], shift, lane)
                others = [ks[i + 1, nxt, :], ks[i + 1, prev, :], ks[i + 2, at, :], ks[i, at, :]]
                faces = [k + other for other in (k_r, k_l, *others)]
                around = [ps[i + 1, nxt, :], ps[i + 1, prev, :], ps[i + 2, at, :], ps[i, at, :]]
                flux = weighted(p, (total_of(faces), faces), (p_r, p_l, *around))
                u_r, u_l = radial_pair(r_ref[0, i, own, :], beside_ref[0, own, :], shift, lane)
                spread = (u_r - u_l) + (ts[i, nxt, :] - ts[i, prev, :])
                spread += zs[i + 2, at, :] - zs[i, at, :]
                if biot_coupling != 2.0:
                    spread = (0.5 * biot_coupling) * spread
                value = (src_ref[i, own, :].astype(f32) + spread) + (storage * p + 0.5 * flux)
                res[h, own, :] = value
                total = total + fold(value * value)
            return total

        sum_ref[...] += lax.fori_loop(0, slab, plane, jnp.zeros((8, width), f32), unroll=8)

    @pl.when(step >= steps)
    def _():
        base = (step - steps) * tile

        def group(j, carry):
            start = pl.multiple_of(base + 8 * j, 8)
            columns = [
                jnp.swapaxes(res[h : h + 8, pl.ds(start, 8), :], 0, 1) for h in range(0, height, 8)
            ]
            for pair in range(4):
                highs, lows = [], []
                for s in range(2):
                    x = jnp.concatenate([column[2 * pair + s] for column in columns], axis=0)
                    high, low = split(x)
                    highs.append(high)
                    lows.append(low)
                high = jnp.concatenate(highs, axis=1)
                low = jnp.concatenate(lows, axis=1)
                stacked = jnp.concatenate([high, low, high], axis=0)
                y = jnp.dot(cos_ref[...], stacked, preferred_element_type=f32)
                for s in range(2):
                    for block, out in enumerate(outs):
                        out[8 * j + 2 * pair + s, :, :] = y[
                            block * levels : (block + 1) * levels, s * width : (s + 1) * width
                        ]
            return carry

        lax.fori_loop(0, tile // 8, group, 0)


def plane_specs(channel, slab, steps, count, width, base=0, part=0):
    at = lambda i: jnp.minimum(i + base, steps - 1)
    up = lambda i: jnp.maximum(at(i) * slab - 1, 0)
    down = lambda i: jnp.minimum(at(i) * slab + slab, steps * slab - 1)
    if channel is None:
        return [
            pl.BlockSpec((slab, count, width), lambda i: (at(i), part, 0)),
            pl.BlockSpec((1, count, width), lambda i: (up(i), part, 0)),
            pl.BlockSpec((1, count, width), lambda i: (down(i), part, 0)),
        ]
    return [
        pl.BlockSpec((1, slab, count, width), lambda i: (channel, at(i), part, 0)),
        pl.BlockSpec((1, 1, count, width), lambda i: (channel, up(i), part, 0)),
        pl.BlockSpec((1, 1, count, width), lambda i: (channel, down(i), part, 0)),
    ]


def fluid(state, source, perm, beside, before, after, table, parts, half, shared):
    _, height, whole_count, width = state.shape
    count = whole_count // HALVES
    steps = height // FLUID
    tile = min(TILE, count)
    pieces = parts * CHUNKS
    levels = height // pieces
    specs = lambda c: plane_specs(c, FLUID, steps, count, width, part=half)
    whole = lambda x: pl.BlockSpec(x.shape, lambda i: (0,) * x.ndim)
    at = lambda first: pl.BlockSpec(
        (tile, levels, width), lambda i: (first + jnp.maximum(i - steps, 0), 0, 0)
    )
    rest = pieces - parts
    return pl.pallas_call(
        functools.partial(fluid_kernel, len(shared)),
        grid=(steps + count // tile,),
        in_specs=[
            *specs(3), *specs(None), *specs(2), specs(0)[0], specs(1)[0], specs(None)[0],
            pl.BlockSpec((6, count, width), lambda i: (0, half, 0)), whole(before), whole(after), whole(table),
            *[pl.BlockSpec(memory_space=pl.ANY)] * len(shared),
        ],
        out_specs=[
            *[at(0)] * parts, *[at(half * (count // tile))] * rest,
            pl.BlockSpec((8, width), lambda i: (0, 0)),
        ],
        out_shape=[
            *[jax.ShapeDtypeStruct((count, levels, width), f32)] * parts,
            *[jax.ShapeDtypeStruct((whole_count, levels, width), f32)] * rest,
            jax.ShapeDtypeStruct((8, width), f32),
        ],
        scratch_shapes=[
            pltpu.VMEM((FLUID + 2, count + 16, width), f32),
            pltpu.VMEM((FLUID + 2, count + 16, width), f32),
            pltpu.VMEM((FLUID + 2, count + 16, width), f32),
            pltpu.VMEM((FLUID, count + 16, width), f32),
            pltpu.VMEM((height, count, width), f32),
            *[pltpu.VMEM((6, height, width), f32)] * 2,
        ],
        input_output_aliases={16 + i: pieces - len(shared) + i for i in range(len(shared))},
        compiler_params=params(),
        name="fluid",
    )(state, state, state, perm, perm, perm, state, state, state, state, state, source,
      beside, before, after, table, *shared)


def momentum_kernel(base, steps, priors, *refs):
    fields = [refs[3 * c : 3 * c + 3] for c in range(5)]
    beside_ref, before_in, after_in = refs[15:18]
    prior_refs = refs[18 : 18 + priors]
    *_, out_ref, rr_ref, rz_ref = refs[:-7]
    *scratch, before_ref, after_ref = refs[-7:]
    step = pl.program_id(0) + base
    _, slab, count, width = out_ref.shape
    height = before_ref.shape[1]

    @pl.when(step == base)
    def _():
        before_ref[...] = before_in[...].astype(f32)
        after_ref[...] = after_in[...].astype(f32)
        rr_ref[...] = total_of([prior[...] for prior in prior_refs[::2]])
        rz_ref[...] = total_of([prior[...] for prior in prior_refs[1::2]])

    for c in range(5):
        center, up, down = fields[c]
        if c < 4:
            center, up, down = center.at[0], up.at[0, 0], down.at[0, 0]
        else:
            up, down = up.at[0], down.at[0]
        stage(scratch[c], center, up, down, before_ref.at[c], after_ref.at[c], step, steps, slab, count)
    lane = lanes_of((ROWS, width))

    def plane(i, totals):
        rr, rz = totals
        h = step * slab + i
        shift = 2 * height - 1 - 2 * h
        for a in range(0, count, ROWS):
            at = slice(8 + a, 8 + a + ROWS)
            prev = slice(7 + a, 7 + a + ROWS)
            nxt = slice(9 + a, 9 + a + ROWS)
            own = slice(a, a + ROWS)

            def around(c):
                s = scratch[c]
                center = fields[c][0].at[0] if c < 4 else fields[c][0]
                right, left = radial_pair(center[i, own, :], beside_ref[c, own, :], shift, lane)
                others = [s[i + 1, nxt, :], s[i + 1, prev, :], s[i + 2, at, :], s[i, at, :]]
                return s[i + 1, at, :], (right, left, *others)

            g, g_around = around(4)
            faces = [g + other for other in g_around]
            diagonal = total_of(faces)
            inverse = -1.0 / diagonal
            _, p = around(3)
            squares = None
            for c in range(3):
                u, u_around = around(c)
                value = weighted(u, (diagonal, faces), u_around)
                value = value + biot_coupling * (p[2 * c] - p[2 * c + 1])
                out_ref[c, i, own, :] = value * inverse
                squares = value * value if squares is None else squares + value * value
            rr = rr + fold(squares)
            rz = rz + fold(squares * inverse)
        return rr, rz

    zero = jnp.zeros((8, width), f32)
    rr, rz = lax.fori_loop(0, slab, plane, (zero, zero), unroll=2)
    rr_ref[...] += 0.25 * rr
    rz_ref[...] -= 0.5 * rz


def momentum(state, shear, beside, before, after, piece, prior, rows=None):
    _, height, count, width = state.shape
    steps = height // SLAB
    base, end = ((eighth * steps) // 8 for eighth in piece)
    specs = lambda c: plane_specs(c, SLAB, steps, count, width, base=base)
    whole = lambda x: pl.BlockSpec(x.shape, lambda i: (0,) * x.ndim)
    operands = [*[state] * 12, shear, shear, shear, beside, before, after, *prior]
    in_specs = [
        *specs(0), *specs(1), *specs(2), *specs(3), *specs(None),
        *[whole(x) for x in operands[15:]],
    ]
    aliases = {}
    if rows is not None:
        aliases = {len(operands): 0}
        operands.append(rows)
        in_specs.append(pl.BlockSpec(memory_space=pl.ANY))
    return pl.pallas_call(
        functools.partial(momentum_kernel, base, steps, len(prior)),
        grid=(end - base,),
        in_specs=in_specs,
        out_specs=[
            pl.BlockSpec((3, SLAB, count, width), lambda i: (0, i + base, 0, 0)),
            pl.BlockSpec((8, width), lambda i: (0, 0)),
            pl.BlockSpec((8, width), lambda i: (0, 0)),
        ],
        out_shape=[
            jax.ShapeDtypeStruct((3, height, count, width), f32),
            jax.ShapeDtypeStruct((8, width), f32),
            jax.ShapeDtypeStruct((8, width), f32),
        ],
        scratch_shapes=[
            *[pltpu.VMEM((SLAB + 2, count + 16, width), f32)] * 5,
            *[pltpu.VMEM((6, height, width), f32)] * 2,
        ],
        input_output_aliases=aliases,
        compiler_params=params(),
        name="momentum",
    )(*operands)


def product(x, high_ref, low_ref):
    high, low = split(x)
    y = jnp.dot(high, high_ref[...], preferred_element_type=f32)
    y = y + jnp.dot(low, high_ref[...], preferred_element_type=f32)
    return y + jnp.dot(high, low_ref[...], preferred_element_type=f32)


def modes_kernel(groups, *refs):
    slabs, (high_ref, low_ref, ratio_ref, x_ref, all_ref, ends_ref, power) = refs[:-7], refs[-7:]
    step = pl.program_id(0)
    tile, levels, width = slabs[0].shape

    @pl.when(step == 0)
    def _():
        ends_ref[...] = jnp.zeros_like(ends_ref)
        power[...] = jnp.ones_like(power)

    each = len(slabs) // groups
    span = pl.num_programs(0) // groups
    for half in range(groups):

        @pl.when((step >= half * span) & (step < (half + 1) * span))
        def _():
            mine = slabs[half * each : (half + 1) * each]
            lines = jnp.concatenate([slab[...].reshape(tile * levels, width) for slab in mine], axis=1)
            x_ref[...] = product(lines, high_ref, low_ref).reshape(x_ref.shape)

    ratio = ratio_ref[...]

    def scan(a, carry):
        forward, backward, weight = carry
        x = x_ref[a]
        return x + ratio * forward, backward + weight * x, weight * ratio

    forward, backward, weight = lax.fori_loop(
        0, tile, scan, (ends_ref[0], ends_ref[1], power[...]), unroll=4
    )
    ends_ref[0] = forward
    ends_ref[1] = backward
    power[...] = weight

    @pl.when(step == pl.num_programs(0) - 1)
    def _():
        for shard in range(all_ref.shape[0]):
            all_ref[shard] = ends_ref[...]


def modes(groups, high, low, ratio, shards):
    slabs = sum(groups, [])
    span, levels, width = slabs[0].shape
    count = span * len(groups)
    tile = min(TILE, span)
    total = high.shape[1]
    steps = span // tile
    at = lambda half: pl.BlockSpec(
        (tile, levels, width), lambda i: (jnp.clip(i - half * steps, 0, steps - 1), 0, 0)
    )
    whole = lambda x: pl.BlockSpec(x.shape, lambda i: (0,) * x.ndim)
    return pl.pallas_call(
        functools.partial(modes_kernel, len(groups)),
        grid=(count // tile,),
        in_specs=[
            *[at(half) for half, group in enumerate(groups) for _ in group],
            whole(high), whole(low), whole(ratio),
        ],
        out_specs=[
            pl.BlockSpec((tile, levels, total), lambda i: (i, 0, 0)),
            pl.BlockSpec((shards, 2, levels, total), lambda i: (0, 0, 0, 0)),
        ],
        out_shape=[
            jax.ShapeDtypeStruct((count, levels, total), f32),
            jax.ShapeDtypeStruct((shards, 2, levels, total), f32),
        ],
        scratch_shapes=[pltpu.VMEM((2, levels, total), f32), pltpu.VMEM((levels, total), f32)],
        compiler_params=params(),
        name="modes",
    )(*slabs, high, low, ratio)


def solve_kernel(
    last, bounds, place_ref, x_ref, ends_ref, ratio_ref, gain_ref, span_ref, high_ref, low_ref,
    rr_ref, rz_ref, prior_ref, *rest,
):
    outs, (all_ref, sum_ref, lines, tail, carry_ref, block) = rest[:-6], rest[-6:]
    step = pl.program_id(0)
    half = pl.num_programs(0) // 2
    shards = ends_ref.shape[0]
    tile, levels, total = x_ref.shape
    width = outs[0].shape[2]
    ratio = ratio_ref[...]

    @pl.when(step == 0)
    def _():
        span = span_ref[...]
        place = place_ref[0]
        weight = jnp.ones_like(span)
        forward = jnp.zeros_like(span)
        backward = jnp.zeros_like(span)
        for j in range(1, shards + 1):
            forward += weight * ends_ref[lax.rem(place - j + shards, shards), 0]
            backward += weight * ends_ref[lax.rem(place + j, shards), 1]
            weight = weight * span
        carry_ref[...] = forward / (1.0 - weight)
        tail[...] = backward / (1.0 - weight)
        sum_ref[...] = jnp.zeros_like(sum_ref)

    @pl.when(step < half)
    def _():
        def scan(a, y):
            y = x_ref[a] + ratio * y
            lines[step * tile + a] = y
            return y

        carry_ref[...] = lax.fori_loop(0, tile, scan, carry_ref[...], unroll=4)

    @pl.when(step == half)
    def _():
        carry_ref[...] = gain_ref[...] * (ratio * carry_ref[...] + tail[...])

    @pl.when(step >= half)
    def _():
        base = (2 * half - 1 - step) * tile

        def scan(j, carry):
            q, dot = carry
            a = tile - 1 - j
            q = ratio * (lines[base + a] + q)
            block[a] = q
            return q, dot + x_ref[a] * q

        zero = jnp.zeros((levels, total), f32)
        q, dot = lax.fori_loop(0, tile, scan, (carry_ref[...], zero), unroll=4)
        carry_ref[...] = q
        sum_ref[...] += dot
        back = product(block[...].reshape(tile * levels, total), high_ref, low_ref)
        for index, out in enumerate(outs):
            group, part = divmod(index, total // width)

            @pl.when((base >= bounds[group]) & (base < bounds[group + 1]))
            def _():
                out[...] = back[:, part * width : (part + 1) * width].reshape(tile, levels, width)

    @pl.when(step == 2 * half - 1)
    def _():
        dots = fold(sum_ref[...])
        lanes = dots[:, :width]
        for start in range(width, total, width):
            lanes = lanes + dots[:, start : start + width]
        sums = lanes + prior_ref[...]
        if last:
            row = lax.broadcasted_iota(jnp.int32, (8, width), 0)
            rr = jnp.sum(rr_ref[...], axis=0, keepdims=True)
            rz = jnp.sum(rz_ref[...] + sums, axis=0, keepdims=True)
            sums = jnp.where(row == 0, rr, jnp.where(row == 1, rz, 0.0))
        for device in range(all_ref.shape[0]):
            all_ref[device] = sums


def solve(place, x, ends, ratio, gain, span, high, low, rr, rz, prior, parts, copies, last):
    count, levels, total = x.shape
    bounds = (0, count // TAIL, count) if last else (0, count)
    groups = len(bounds) - 1
    tile = min(TILE, count // TAIL)
    half = count // tile
    width = total // parts
    whole = lambda v: pl.BlockSpec(v.shape, lambda i, s: (0,) * v.ndim)
    back = lambda i: jnp.minimum(2 * half - 1 - i, half - 1)
    out_at = lambda group: pl.BlockSpec(
        (tile, levels, width),
        lambda i, s: (jnp.clip(back(i), bounds[group] // tile, bounds[group + 1] // tile - 1) - bounds[group] // tile, 0, 0),
    )
    return pl.pallas_call(
        functools.partial(solve_kernel, last, bounds),
        grid_spec=pltpu.PrefetchScalarGridSpec(
            num_scalar_prefetch=1,
            grid=(2 * half,),
            in_specs=[
                pl.BlockSpec((tile, levels, total), lambda i, s: (jnp.minimum(i, 2 * half - 1 - i), 0, 0)),
                whole(ends), whole(ratio), whole(gain), whole(span), whole(high), whole(low), whole(rr), whole(rz), whole(prior),
            ],
            out_specs=[
                *[out_at(group) for group in range(groups) for _ in range(parts)],
                pl.BlockSpec((copies, 8, width), lambda i, s: (0, 0, 0)),
            ],
            scratch_shapes=[
                pltpu.VMEM((levels, total), f32),
                pltpu.VMEM((count, levels, total), f32),
                pltpu.VMEM((levels, total), f32),
                pltpu.VMEM((levels, total), f32),
                pltpu.VMEM((tile, levels, total), f32),
            ],
        ),
        out_shape=[
            *[
                jax.ShapeDtypeStruct((bounds[group + 1] - bounds[group], levels, width), f32)
                for group in range(groups) for _ in range(parts)
            ],
            jax.ShapeDtypeStruct((copies, 8, width), f32),
        ],
        compiler_params=params(),
        name="solve",
    )(place, x, ends, ratio, gain, span, high, low, rr, rz, prior)


def scale_kernel(alpha_ref, in_ref, out_ref):
    out_ref[...] = (alpha_ref[0] * in_ref[...]).astype(bf16)


def scale_rows(alpha, moment):
    _, height, count, width = moment.shape
    return pl.pallas_call(
        scale_kernel,
        grid_spec=pltpu.PrefetchScalarGridSpec(
            num_scalar_prefetch=1,
            grid=(3 * height // 16,),
            in_specs=[pl.BlockSpec((1, 16, count, width), lambda i, s: (i // (height // 16), i % (height // 16), 0, 0))],
            out_specs=pl.BlockSpec((1, 16, count, width), lambda i, s: (i // (height // 16), i % (height // 16), 0, 0)),
        ),
        out_shape=jax.ShapeDtypeStruct((4, height, count, width), bf16),
        compiler_params=params(),
        name="scale_rows",
    )(alpha, moment)


def pressure_kernel(alpha_ref, *refs):
    pieces, (cos_ref, rest_ref, out_ref) = refs[:-3], refs[-3:]
    tile, levels, width = pieces[0].shape
    height = levels * len(pieces)
    alpha = alpha_ref[0]

    def group(j, carry):
        planes = []
        for pair in range(8):
            highs, lows = [], []
            for s in range(2):
                a = 16 * j + 2 * pair + s
                x = jnp.concatenate([piece[a] for piece in pieces], axis=0)
                high, low = split(x)
                highs.append(high)
                lows.append(low)
            high = jnp.concatenate(highs, axis=1)
            low = jnp.concatenate(lows, axis=1)
            stacked = jnp.concatenate([high, low, high], axis=0)
            y = alpha * jnp.dot(cos_ref[...], stacked, preferred_element_type=f32)
            planes += [y[:, :width], y[:, width:]]
        start = pl.multiple_of(16 * j, 16)
        for h in range(0, height, 8):
            low = jnp.swapaxes(jnp.stack([y[h : h + 8] for y in planes[:8]]), 0, 1)
            high = jnp.swapaxes(jnp.stack([y[h : h + 8] for y in planes[8:]]), 0, 1)
            block = jnp.concatenate([low, high], axis=1)
            out_ref[0, h : h + 8, pl.ds(start, 16), :] = block.astype(bf16)
        return carry

    lax.fori_loop(0, tile // 16, group, 0)


def pressure_rows(alpha, planes, table, out, half):
    _, height, whole_count, width = out.shape
    count = planes[-1].shape[0]
    tile = min(32, whole_count // TAIL)
    first = half * (whole_count // TAIL // tile)
    at = lambda x: pl.BlockSpec(
        (tile, *x.shape[1:]), lambda i, s: (i if x.shape[0] == count else first + i, 0, 0)
    )
    return pl.pallas_call(
        pressure_kernel,
        grid_spec=pltpu.PrefetchScalarGridSpec(
            num_scalar_prefetch=1,
            grid=(count // tile,),
            in_specs=[
                *[at(x) for x in planes],
                pl.BlockSpec(table.shape, lambda i, s: (0, 0)),
                pl.BlockSpec(memory_space=pl.ANY),
            ],
            out_specs=pl.BlockSpec((1, height, tile, width), lambda i, s: (3, 0, first + i, 0)),
        ),
        out_shape=jax.ShapeDtypeStruct(out.shape, bf16),
        input_output_aliases={len(planes) + 2: 0},
        compiler_params=params(),
        name="pressure_rows",
    )(alpha, *planes, table, out)


def cosine_table(extent):
    row_ids = jnp.arange(extent, dtype=f32)[:, None]
    col_ids = jnp.arange(extent, dtype=f32)[None, :]
    scaled = jnp.where(row_ids == 0, math.sqrt(1.0 / extent), math.sqrt(2.0 / extent))
    return scaled * jnp.cos(math.pi * (col_ids + 0.5) * row_ids / extent)


def pairwise(pieces, axis):
    count = lax.axis_size(axis)
    return [pieces[0]] + [
        lax.ppermute(pieces[s], axis, [(i, i ^ s) for i in range(count)]) for s in range(1, count)
    ]


def exchanged(copies, axis):
    return lax.all_to_all(copies, axis, split_axis=0, concat_axis=0, tiled=True)


def fence(*values):
    return lax.optimization_barrier(values)


def step(state, source, shear, permeability, radial_basis, radial_eigen):
    _, height, count, width = state.shape
    parts = lax.axis_size("rad")
    levels = height // parts // CHUNKS
    owner = lax.axis_index("rad") ^ jnp.arange(parts, dtype=jnp.int32)
    cosine = cosine_table(height).reshape(parts, CHUNKS, levels, height)
    cosine = jnp.swapaxes(jnp.take(cosine, owner, axis=0), 0, 1).reshape(height, height)
    high, low = split_table(cosine)
    table = jnp.concatenate([high, high, low], axis=1)

    cols, first, *others = edges(state, shear, permeability)
    first, radial_basis = fence(first, radial_basis)
    beside, before, after, mid_low, mid_high = neighbours(cols, first, *others)
    blocks = pairwise([radial_basis] * parts, "rad")
    sent, priors, shared = [], [], []
    for half, ends in enumerate(((before, mid_high), (mid_low, after))):
        *heights, fluid_rr = fluid(
            state, source, permeability, beside, *ends, table, parts, half, shared
        )
        shared = heights[parts:]
        sent.append(pairwise(heights[:parts], "rad"))
        priors += [fluid_rr, jnp.zeros_like(fluid_rr)]
    slabs = [sent]
    for chunk in range(1, CHUNKS):
        slabs.append([pairwise(shared[(chunk - 1) * parts : chunk * parts], "rad")])
    high, low = split_table(jnp.concatenate(blocks))
    around = (beside, before, after)
    moment, rr, rz = momentum(state, shear, *around, (0, 3), priors)

    place = lax.axis_index("az").reshape(1)
    shards = lax.axis_size("az")
    sums = jnp.zeros((8, width), f32)
    planes = []
    for chunk in range(CHUNKS):
        first = (lax.axis_index("rad") * CHUNKS + chunk) * levels
        level = (first + jnp.arange(levels, dtype=jnp.int32)).astype(f32)
        height_eigen = 4.0 * jnp.sin(math.pi * level / (2.0 * height)) ** 2
        center = storage + radial_eigen[None, :] + height_eigen[:, None]
        root = jnp.sqrt(center * (center + 4.0))
        ratio = 2.0 / (center + 2.0 + root)
        span = lax.integer_pow(ratio, count)
        x, ends = modes(slabs[chunk], high, low, ratio, shards)
        ends = exchanged(ends, "az")
        piece = ((3, 4), (6, 8))[chunk]
        moment, rr, rz = momentum(state, shear, *around, piece, (rr, rz), moment)
        last = chunk == CHUNKS - 1
        copies = shards * parts if last else 1
        *back, sums = solve(
            place, x, ends, ratio, 1.0 / root, span, high.T, low.T, rr, rz, sums, parts, copies, last
        )
        if last:
            sums = exchanged(sums, ("az", "rad"))
        else:
            sums = sums[0]
            moment, rr, rz = momentum(state, shear, *around, (4, 6), (rr, rz), moment)
        if last:
            backs = [None] * HALVES
            for half in reversed(range(HALVES)):
                backs[half] = pairwise(back[half * parts : (half + 1) * parts], "rad")
        else:
            planes += pairwise(back, "rad")
    totals = jnp.sum(sums, axis=(0, 2))
    alpha = (totals[0] / totals[1]).reshape(1)
    out = scale_rows(alpha, moment)
    high, low = split_table(cosine.T)
    table = jnp.concatenate([high, high, low], axis=1)
    for half in reversed(range(HALVES)):
        out = pressure_rows(alpha, planes + backs[half], table, out, half)
    return out


def solution(mesh):
    placed = (
        P(None, None, "az", "rad"),
        P(None, "az", "rad"),
        P(None, "az", "rad"),
        P(None, "az", "rad"),
        P("rad", None),
        P(),
    )
    return jax.shard_map(
        step, mesh=mesh, in_specs=placed, out_specs=P(None, None, "az", "rad"), check_vma=False
    )
```
